32 devices in a mesh: reg: 16 (over z, y, x), col: 2 (over core).
Axes of the slice: x: 2, y: 2, z: 4, core: 2. Of those that a mesh axis runs over, the one named last changes fastest.
Arguments:
- innovation: float32 [64, 131072], P(None, ('reg', 'col')), may hold values from -6 to 6
- obs_along: float32 [131072], P(('reg', 'col')), may hold values from 0 to 2
- obs_across: float32 [131072], P(('reg', 'col')), may hold values from 0 to 32
- obs_scale: float32 [131072], P(('reg', 'col')), may hold values from 0.5 to 2
- obs_error: float32 [131072], P(('reg', 'col')), may hold values from 0.1 to 1
- obs_gain: float32 [131072], P(('reg', 'col')), may hold values from 0.3 to 3
- pair_live: int32 [128, 2], P(('reg', 'col')), may hold values 0 or 1
- obs_count: int32 [128], P(('reg', 'col')), may hold values from 256 to 1024, as said below
- col_owner: int32 [131072], P(('reg', 'col')), may hold values from 0 to 32767, as said below
Outputs:
- weights: float32 [64, 131072], P(None, ('reg', 'col'))
- increments: float32 [64, 32768], P(None, ('reg', 'col'))
The draws below stay inside these ranges and needn't reach their ends.
Inputs may be any that keep to these rules, and one draw needn't show every extreme that they name: `obs_count`: slots of a region block at or after its count are empty. Some region holds 1024 observations and some holds 256. `col_owner`: observation slot o lies in device block k = o // 4096, and its column is one of k * 1024 to k * 1024 + 2 * 1024 - 1, taken modulo 32768; column block k belongs to the same position k in the order of devices.
All inputs are finite; a program needn't handle non-finite values. No bound on the sum of `pair_live` on one device may be relied on, other than what follows from the above.
Results may differ from the reference program's by a relative error of at most 0.0003.
Values sent between devices are 32-bit elements; how exact they have to be, the bound alone decides.
A program may use at most 64 MiB of HBM per device.

```python
import math
import jax
import jax.numpy as jnp
from jax import lax

ENS = 64
ROWS = 1024
REACH = 2
ITERS = 2
REG_DEV = 4
COLS_DEV = 1024
NREG = 128
NOBS = 131072
NCOL = 32768


def draw_obs_count(key, part):
    counts = jax.random.randint(jax.random.fold_in(key, 11), (NREG,), ROWS // 4, ROWS + 1)
    full_region = jax.random.randint(jax.random.fold_in(key, 12), (), 0, NREG)
    shift_draw = jax.random.randint(jax.random.fold_in(key, 13), (), 1, NREG)
    least_region = (full_region + shift_draw) % NREG
    region_ids = jnp.arange(NREG, dtype=jnp.int32)
    counts = jnp.where(region_ids == full_region, ROWS, counts)
    counts = jnp.where(region_ids == least_region, ROWS // 4, counts)
    return counts.astype(jnp.int32)


def draw_col_owner(key, part):
    owner_block = jnp.arange(NOBS, dtype=jnp.int32) // (REG_DEV * ROWS)
    offset_draw = jax.random.randint(jax.random.fold_in(key, 21), (NOBS,), 0, 2 * COLS_DEV)
    return ((owner_block * COLS_DEV + offset_draw) % NCOL).astype(jnp.int32)


def set_ends(values, rng, smallest, largest):
    place = [jax.random.randint(jax.random.fold_in(rng, axis), (), 0, length) for axis, length in enumerate(values.shape)]
    main_axis = values.shape.index(max(values.shape))
    neighbour = place[:main_axis] + [(place[main_axis] + 1) % values.shape[main_axis]] + place[main_axis + 1:]
    return values.at[tuple(place)].set(smallest).at[tuple(neighbour)].set(largest)


def shard_levels(rng, shape, shards, least, top_value):
    factor_of = 1.0
    for dim, blocks in shards:
        heights = jax.random.uniform(jax.random.fold_in(jax.random.fold_in(rng, 6), dim), (blocks,), jnp.float32, least / len(shards), top_value / len(shards))
        factor_of = factor_of * jnp.repeat(jnp.exp(heights), shape[dim] // blocks).reshape((-1,) + (1,) * (len(shape) - 1 - dim))
    return factor_of


def gaussian(rng, dims, scale, bound, shards=(), held_as=jnp.bfloat16):
    result = scale * jax.random.normal(rng, dims, jnp.float32)
    if shards:
        result = result * shard_levels(rng, dims, shards, -0.22, 0.18)
    return jnp.clip(result, -bound, bound).astype(held_as)


def setup_inputs(seed: int = 0) -> dict:
    streams_of = jax.random.split(jax.random.key(seed), 10)
    return {
        "innovation": gaussian(streams_of[0], (ENS, NOBS), 1.0, 6.0, ((1, 32),), jnp.float32),
        "obs_along": jnp.clip(2.0 * jax.random.uniform(streams_of[1], (NOBS,), jnp.float32) ** shard_levels(streams_of[1], (NOBS,), ((0, 32),), -0.2, 0.2), 0.0, 2.0),
        "obs_across": jnp.clip(32.0 * jax.random.uniform(streams_of[2], (NOBS,), jnp.float32) ** shard_levels(streams_of[2], (NOBS,), ((0, 32),), -0.2, 0.2), 0.0, 32.0),
        "obs_scale": jnp.clip(jnp.exp(math.log(2.0) - 1.3862944 * jax.random.uniform(streams_of[3], (NOBS,), jnp.float32) ** shard_levels(streams_of[3], (NOBS,), ((0, 32),), -0.2, 0.2)), 0.5, 2.0),
        "obs_error": jnp.clip(jnp.exp(math.log(1.0) - 2.3025851 * jax.random.uniform(streams_of[4], (NOBS,), jnp.float32) ** shard_levels(streams_of[4], (NOBS,), ((0, 32),), -0.2, 0.2)), 0.1, 1.0),
        "obs_gain": jnp.clip(jnp.exp(math.log(3.0) - 2.3025851 * jax.random.uniform(streams_of[5], (NOBS,), jnp.float32) ** shard_levels(streams_of[5], (NOBS,), ((0, 32),), -0.2, 0.2)), 0.3, 3.0),
        "pair_live": set_ends((jax.random.randint(streams_of[6], (NREG, REACH), 0, 4) < 3).astype(jnp.int32), jax.random.fold_in(streams_of[6], 1), 0, 1),
        "obs_count": draw_obs_count(jax.random.fold_in(streams_of[9], 71), 0),
        "col_owner": draw_col_owner(jax.random.fold_in(streams_of[9], 71), 0),
    }


support_radius = 1.0
norm_scale = 16.0
highest = lax.Precision.HIGHEST

def support_shape(row_along, row_across, col_along, col_across, offset):
    delta_along = offset + col_along[None, :] - row_along[:, None]
    delta_across = col_across[None, :] - row_across[:, None]
    scaled_dist = jnp.minimum(jnp.sqrt(delta_along * delta_along + delta_across * delta_across) / support_radius, 1.0)
    return (1.0 - scaled_dist) ** 4 * (4.0 * scaled_dist + 1.0)

def cov_block(row_meta, col_meta, offset, factor):
    shape_part = support_shape(row_meta[0], row_meta[1], col_meta[0], col_meta[1], offset)
    return row_meta[2][:, None] * col_meta[2][None, :] * (shape_part * (factor / norm_scale))

def gram_matrix(lhs_rows, rhs_rows):
    return lax.dot_general(lhs_rows.astype(jnp.float32), rhs_rows.astype(jnp.float32), (((1,), (1,)), ((), ())), precision=highest, preferred_element_type=jnp.float32)

def combine_rows(coefficients, blocks):
    return lax.dot_general(coefficients.astype(jnp.float32), blocks.astype(jnp.float32), (((0,), (0,)), ((), ())), precision=highest, preferred_element_type=jnp.float32)

def symmetric(matrix):
    return 0.5 * (matrix + matrix.T)

def spd_solve(matrix, right_side):
    lower_factor = jnp.linalg.cholesky(matrix)
    return jax.scipy.linalg.cho_solve((lower_factor, True), right_side)

def operate(vectors, obs_along, obs_across, weight, factors, obs_error):
    blocks = vectors.reshape(ENS, NREG, ROWS)
    along_blocks = obs_along.reshape(NREG, ROWS)
    across_blocks = obs_across.reshape(NREG, ROWS)
    weight_blocks = weight.reshape(NREG, ROWS)
    summed = (obs_error[None, :] * vectors).reshape(ENS, NREG, ROWS)
    for offset in range(REACH + 1):

        def one_pair(region, offset=offset):
            partner = (region + offset) % NREG
            row_meta = (along_blocks[region], across_blocks[region], weight_blocks[region])
            col_meta = (along_blocks[partner], across_blocks[partner], weight_blocks[partner])
            factor = 1.0 if offset == 0 else factors[region, offset - 1]
            cov_tile = cov_block(row_meta, col_meta, offset, factor)
            to_self = gram_matrix(blocks[:, partner], cov_tile)
            if offset == 0:
                return (to_self, to_self)
            to_partner = jnp.dot(blocks[:, region].astype(jnp.float32), cov_tile.astype(jnp.float32), precision=highest, preferred_element_type=jnp.float32)
            return (to_self, to_partner)
        to_self, to_partner = lax.map(one_pair, jnp.arange(NREG, dtype=jnp.int32))
        summed = summed + jnp.transpose(to_self, (1, 0, 2))
        if offset > 0:
            summed = summed + jnp.transpose(jnp.roll(to_partner, offset, axis=0), (1, 0, 2))
    return summed.reshape(ENS, NOBS)

def reference(innovation, obs_along, obs_across, obs_scale, obs_error, obs_gain, pair_live, obs_count, col_owner):
    live_mask = (jnp.arange(ROWS, dtype=jnp.int32)[None, :] < obs_count[:, None]).astype(jnp.float32).reshape(NOBS)
    weight = obs_scale * live_mask
    factors = pair_live.astype(jnp.float32)
    residual = innovation * live_mask[None, :]
    solution = jnp.zeros_like(residual)
    direction = residual
    norm_now = symmetric(gram_matrix(residual, residual))
    for iteration in range(ITERS):
        images = operate(direction, obs_along, obs_across, weight, factors, obs_error)
        curvature = symmetric(gram_matrix(direction, images))
        step_size = spd_solve(curvature, norm_now)
        solution = solution + combine_rows(step_size, direction)
        residual = residual - combine_rows(step_size, images)
        if iteration + 1 < ITERS:
            norm_next = symmetric(gram_matrix(residual, residual))
            conjugate = spd_solve(norm_now, norm_next)
            direction = residual + combine_rows(conjugate, direction)
            norm_now = norm_next
    scaled = solution * obs_gain[None, :]
    increments = jax.ops.segment_sum(scaled.T, col_owner, num_segments=NCOL).T
    return (solution, increments)
```

```python
import functools

import jax
import jax.numpy as jnp
from jax import lax
from jax.experimental import pallas as pl
from jax.experimental.pallas import tpu as pltpu
from jax.sharding import PartitionSpec as P

ROWS = 1024
REACH = 2
COLS_DEV = 1024
META = 16
KB = 128
NB = 256
DEAD = 1e9
VMEM_LIMIT = 60 * 1024 * 1024

highest = lax.Precision.HIGHEST
f32 = jnp.float32
bf16 = jnp.bfloat16
NT = (((1,), (1,)), ((), ()))
NN = (((1,), (0,)), ((), ()))
TN = (((0,), (0,)), ((), ()))
vmem = pl.BlockSpec(memory_space=pltpu.VMEM)
smem = pl.BlockSpec(memory_space=pltpu.SMEM)


def shift(block, distance):
    axis = ("reg", "col")
    n = lax.axis_size(axis)
    return lax.ppermute(block, axis, [((i - distance) % n, i) for i in range(n)])


def dot(a, b, dims=NN):
    return lax.dot_general(a, b, dims, preferred_element_type=f32)


def two(x):
    hi = x.astype(bf16)
    return hi, (x - hi.astype(f32)).astype(bf16)


def three(x):
    hi = x.astype(bf16)
    rest = x - hi.astype(f32)
    mid = rest.astype(bf16)
    return hi, mid, (rest - mid.astype(f32)).astype(bf16)


def combine(coef_t, blocks):
    chi, clo = two(coef_t)
    bhi, blo = two(blocks)
    return dot(
        jnp.concatenate([chi, chi, clo], axis=1), jnp.concatenate([bhi, blo, bhi], axis=0)
    )


def params():
    return pltpu.CompilerParams(vmem_limit_bytes=VMEM_LIMIT)


def sort_kernel(innov_ref, meta_ref, out_ref, rank_ref):
    regions = innov_ref.shape[1] // ROWS

    def one(g, carry):
        cols = pl.ds(pl.multiple_of(g * ROWS, ROWS), ROWS)
        meta = meta_ref[:, cols]
        key = meta[6:7]
        live = (key < 0.5 * DEAD).astype(f32)
        key_col = jnp.broadcast_to(key, (128, ROWS)).T
        ranks = []
        sub = lax.broadcasted_iota(jnp.int32, (ROWS, 128), 0)
        lane = lax.broadcasted_iota(jnp.int32, (ROWS, 128), 1)
        for b in range(ROWS // 128):
            mine = key[:, b * 128 : (b + 1) * 128]
            before = (key_col < mine) | ((key_col == mine) & (sub < lane + b * 128))
            ranks.append(jnp.sum(before.astype(f32), axis=0, keepdims=True))
        rank = jnp.concatenate(ranks, axis=1)
        rank_ref[:, cols] = jnp.broadcast_to(rank, (8, ROWS))
        stack = jnp.concatenate([innov_ref[:, cols] * live, meta], axis=0)
        lhs = jnp.concatenate(three(stack), axis=0)
        n = stack.shape[0]
        rank_i = rank.astype(jnp.int32)
        for c in range(ROWS // 256):
            slot = lax.broadcasted_iota(jnp.int32, (256, ROWS), 0) + c * 256
            place = (slot == rank_i).astype(f32).astype(bf16)
            got = dot(lhs, place, NT)
            start = pl.multiple_of(g * ROWS + c * 256, 256)
            out_ref[:, pl.ds(start, 256)] = got[:n] + got[n : 2 * n] + got[2 * n :]
        return carry

    lax.fori_loop(0, regions, one, 0)


def sort_call(innov, meta):
    n = innov.shape[1]
    return pl.pallas_call(
        sort_kernel,
        out_shape=(
            jax.ShapeDtypeStruct((innov.shape[0] + META, n), f32),
            jax.ShapeDtypeStruct((8, n), f32),
        ),
        in_specs=[vmem, vmem],
        out_specs=(vmem, vmem),
        compiler_params=params(),
        name="sort_slots",
    )(innov, meta)


def apply_cov(bounds_ref, row_ref, col_ref, v_ref, img_ref, stack_ref):
    ens, wide = v_ref.shape
    own = img_ref.shape[1]
    lead = REACH * ROWS
    tiles = own // NB
    per = ROWS // NB
    chunk = 2048
    for c in range(wide // chunk):
        at = pl.ds(c * chunk, chunk)
        hi, lo = two(v_ref[:, at] * row_ref[2:3, at])
        stack_ref[0:ens, at] = hi
        stack_ref[ens : 2 * ens, at] = lo

    def one(t, carry):
        g = t // per
        i_at = pl.ds(pl.multiple_of(lead + t * NB, NB), NB)
        a_i = row_ref[0:1, i_at]
        b_i = row_ref[1:2, i_at]

        def step(dh, jb, acc):
            start = pl.multiple_of((g + dh) * ROWS + jb * KB, KB)
            j_at = pl.ds(start, KB)
            da = col_ref[j_at, 0:1] - a_i
            db = col_ref[j_at, 1:2] - b_i
            r2 = da * da + db * db
            u = jnp.maximum(1.0 - r2 * lax.rsqrt(jnp.maximum(r2, 1e-30)), 0.0)
            u2 = u * u
            s = (u2 * u2) * (5.0 - 4.0 * u)
            shi, slo = two(s)
            vs = stack_ref[:, j_at]
            return (acc[0] + dot(vs, shi), acc[1] + dot(vs[:ens], slo))

        acc = (jnp.zeros((2 * ens, NB), f32), jnp.zeros((ens, NB), f32))
        for dh in range(2 * REACH + 1):
            lo = bounds_ref[0, dh * tiles + t]
            hi = bounds_ref[1, dh * tiles + t]
            acc = lax.fori_loop(lo, hi, functools.partial(step, dh), acc)
        total = acc[0][:ens] + acc[0][ens:] + acc[1]
        o_at = pl.ds(pl.multiple_of(t * NB, NB), NB)
        img_ref[:, o_at] = total * (row_ref[2:3, i_at] * 0.0625) + row_ref[3:4, i_at] * v_ref[:, i_at]
        return carry

    lax.fori_loop(0, tiles, one, 0)


def gram(a, b):
    return lax.dot_general(a, b, NT, precision=highest, preferred_element_type=f32)


def first_kernel(bounds_ref, row_ref, col_ref, v_ref, img_ref, gram_ref, stack_ref):
    ens = v_ref.shape[0]
    own = img_ref.shape[1]
    lead = REACH * ROWS
    apply_cov(bounds_ref, row_ref, col_ref, v_ref, img_ref, stack_ref)
    r = v_ref[:, lead : lead + own]
    gram_ref[0] = gram(r, r)
    gram_ref[1] = gram(r, img_ref[...])


def second_kernel(
    bounds_ref, row_ref, col_ref, step_ref, r0_ref, img0_ref, gram_ref, img_ref, v_ref, stack_ref
):
    own = img_ref.shape[1]
    lead = REACH * ROWS
    chunk = 2048
    step_t = step_ref[...].T
    for c in range(v_ref.shape[1] // chunk):
        at = pl.ds(c * chunk, chunk)
        v_ref[:, at] = r0_ref[:, at] - combine(step_t, img0_ref[:, at])
    apply_cov(bounds_ref, row_ref, col_ref, v_ref, img_ref, stack_ref)
    r = v_ref[:, lead : lead + own]
    gram_ref[0] = gram(r, r)
    gram_ref[1] = gram(r, img_ref[...])
    gram_ref[2] = gram(r, img0_ref[:, lead : lead + own])


def first_call(bounds, row, col, v, own):
    ens, wide = v.shape
    return pl.pallas_call(
        first_kernel,
        out_shape=(
            jax.ShapeDtypeStruct((ens, own), f32),
            jax.ShapeDtypeStruct((2, ens, ens), f32),
        ),
        in_specs=[smem, vmem, vmem, vmem],
        out_specs=(vmem, vmem),
        scratch_shapes=[pltpu.VMEM((2 * ens, wide), bf16)],
        compiler_params=params(),
        name="operate_first",
    )(bounds, row, col, v)


def second_call(bounds, row, col, step, r0, img0, own):
    ens, wide = r0.shape
    return pl.pallas_call(
        second_kernel,
        out_shape=jax.ShapeDtypeStruct((3, ens, ens), f32),
        in_specs=[smem, vmem, vmem, vmem, vmem, vmem],
        out_specs=vmem,
        scratch_shapes=[
            pltpu.VMEM((ens, own), f32),
            pltpu.VMEM((ens, wide), f32),
            pltpu.VMEM((2 * ens, wide), bf16),
        ],
        compiler_params=params(),
        name="operate_second",
    )(bounds, row, col, step, r0, img0)


def columns_kernel(innov_ref, info_ref, rank_ref, img_ref, back_ref, cols_ref):
    ens, own = innov_ref.shape
    regions = own // ROWS
    cols_ref[...] = jnp.zeros_like(cols_ref)

    def one(g, carry):
        at = pl.ds(pl.multiple_of(g * ROWS, ROWS), ROWS)
        rank = rank_ref[0:1, at].astype(jnp.int32)
        lhs = jnp.concatenate(two(img_ref[:, at]), axis=0)
        total = jnp.zeros((2 * ens, ROWS), f32)
        for c in range(ROWS // 256):
            slot = lax.broadcasted_iota(jnp.int32, (256, ROWS), 0) + c * 256
            place = (slot == rank).astype(f32).astype(bf16)
            total = total + dot(lhs[:, c * 256 : (c + 1) * 256], place)
        image = total[:ens] + total[ens:]
        back_ref[:, at] = image
        gain = info_ref[0:1, at]
        live = info_ref[1:2, at]
        owner = info_ref[2:3, at].astype(jnp.int32)
        rhi, rlo = two(innov_ref[:, at] * (gain * live))
        ihi, ilo = two(image * gain)
        stack = jnp.concatenate([rhi, ihi, rlo, ilo], axis=0)
        for c in range(2 * COLS_DEV // 256):
            slot = lax.broadcasted_iota(jnp.int32, (256, ROWS), 0) + c * 256
            hot = (slot == owner).astype(f32).astype(bf16)
            got = dot(stack, hot, NT)
            part = pl.ds(c * 256, 256)
            cols_ref[:, part] += got[: 2 * ens] + got[2 * ens :]
        return carry

    lax.fori_loop(0, regions, one, 0)


def columns_call(innov, info, rank, img):
    ens, own = innov.shape
    return pl.pallas_call(
        columns_kernel,
        out_shape=(
            jax.ShapeDtypeStruct((ens, own), f32),
            jax.ShapeDtypeStruct((2 * ens, 2 * COLS_DEV), f32),
        ),
        in_specs=[vmem] * 4,
        out_specs=(vmem, vmem),
        compiler_params=params(),
        cost_estimate=pl.CostEstimate(
            flops=2 * 256 * own * 3072, bytes_accessed=4 << 20, transcendentals=0
        ),
        name="columns",
    )(innov, info, rank, img)


def final_kernel(coef_ref, innov_ref, info_ref, back_ref, cols_ref, came_ref, w_ref, inc_ref):
    coef = coef_ref[...]
    ens = coef.shape[0]
    own = innov_ref.shape[1]
    chunk = 1024
    first, second = coef[:, :ens], coef[:, ens:]
    for c in range(own // chunk):
        at = pl.ds(c * chunk, chunk)
        live = info_ref[1:2, at]
        w_ref[:, at] = combine(first, innov_ref[:, at] * live) + combine(second, back_ref[:, at])
    both = cols_ref[:, :COLS_DEV] + came_ref[...]
    inc_ref[...] = combine(first, both[:ens]) + combine(second, both[ens:])


def final_call(coef, innov, info, back, cols, came):
    ens, own = innov.shape
    return pl.pallas_call(
        final_kernel,
        out_shape=(
            jax.ShapeDtypeStruct((ens, own), f32),
            jax.ShapeDtypeStruct((ens, COLS_DEV), f32),
        ),
        in_specs=[vmem] * 6,
        out_specs=(vmem, vmem),
        compiler_params=params(),
        name="final",
    )(coef, innov, info, back, cols, came)


def symmetric(matrix):
    return 0.5 * (matrix + matrix.T)


def mm(a, b):
    return jnp.dot(a, b, precision=highest)


def spd_solve(matrix, right_side):
    lower_factor = jnp.linalg.cholesky(matrix)
    return jax.scipy.linalg.cho_solve((lower_factor, True), right_side)


def block_bounds(key_ext, flags_ext, regions):
    wide = regions + 2 * REACH
    jkeys = key_ext.reshape(wide, ROWS // KB, KB)
    jmin = jkeys.min(axis=2)
    jmax = jnp.where(jkeys < 0.5 * DEAD, jkeys, -DEAD).max(axis=2)
    ikeys = key_ext.reshape(wide, ROWS // NB, NB)[REACH : REACH + regions]
    imin = ikeys.min(axis=2)
    imax = jnp.where(ikeys < 0.5 * DEAD, ikeys, -DEAD).max(axis=2)
    los, his = [], []
    ids = jnp.arange(ROWS // KB, dtype=jnp.int32)[None, None, :]
    for dh in range(2 * REACH + 1):
        lo_j = jmin[dh : dh + regions]
        hi_j = jmax[dh : dh + regions]
        d = dh - REACH
        if d == 0:
            flag = jnp.ones((regions,), jnp.bool_)
        elif d > 0:
            flag = flags_ext[d - 1, REACH : REACH + regions] > 0.5
        else:
            flag = flags_ext[-d - 1, REACH + d : REACH + d + regions] > 0.5
        near = (
            (hi_j[:, None, :] >= imin[:, :, None] - 1.001)
            & (lo_j[:, None, :] <= imax[:, :, None] + 1.001)
            & (imin[:, :, None] < 0.5 * DEAD)
            & flag[:, None, None]
        )
        los.append(jnp.where(near, ids, ROWS // KB).min(axis=2).reshape(-1))
        his.append(jnp.where(near, ids + 1, 0).max(axis=2).reshape(-1))
    return jnp.stack([jnp.concatenate(los), jnp.concatenate(his)])


def on_device(
    innovation,
    obs_along,
    obs_across,
    obs_scale,
    obs_error,
    obs_gain,
    pair_live,
    obs_count,
    col_owner,
):
    axes = ("reg", "col")
    regions = obs_count.shape[0]
    ens, own = innovation.shape
    halo = REACH * ROWS
    live = (
        (jnp.arange(ROWS, dtype=jnp.int32)[None, :] < obs_count[:, None])
        .astype(f32)
        .reshape(own)
    )
    flags = jnp.repeat(pair_live.astype(f32).T, ROWS, axis=1)
    zero = jnp.zeros((own,), f32)
    meta = jnp.stack(
        [obs_along, obs_across, obs_scale * live, obs_error, flags[0], flags[1]]
        + [jnp.where(live > 0.5, obs_across, DEAD)]
        + [zero] * (META - 7)
    )
    total_cols = COLS_DEV * lax.axis_size(axes)
    local_col = (col_owner - lax.axis_index(axes) * COLS_DEV) % total_cols
    info = jnp.stack([obs_gain, live, local_col.astype(f32)] + [zero] * 5)

    ordered, rank = sort_call(innovation, meta)
    after = shift(ordered[:, :halo], -1)
    before = shift(ordered[:, own - halo :], 1)
    ext = jnp.concatenate([before, ordered, after], axis=1)
    r0 = ext[:ens]
    region_ids = jnp.repeat(jnp.arange(regions + 2 * REACH, dtype=f32), ROWS)
    row = ext[ens : ens + 8]
    row = row.at[0].add(region_ids)
    col = row.T
    bounds = block_bounds(row[6], row[4:6, ::ROWS], regions)

    img0, grams = first_call(bounds, row, col, r0, own)
    grams = lax.psum(grams, axes)
    img_after = shift(img0[:, :halo], -1)
    img_before = shift(img0[:, own - halo :], 1)
    img_ext = jnp.concatenate([img_before, img0, img_after], axis=1)
    back, cols = columns_call(innovation, info, rank, img0)
    came = shift(cols[:, COLS_DEV:], 1)
    norm0 = symmetric(grams[0])
    curv0 = symmetric(grams[1])
    step0 = spd_solve(curv0, norm0)
    grams = lax.psum(second_call(bounds, row, col, step0, r0, img_ext, own), axes)
    norm1 = symmetric(grams[0])
    conj = spd_solve(norm0, norm1)
    coupled = mm(grams[2], conj)
    curv1 = symmetric(grams[1] + coupled + coupled.T + mm(conj.T, mm(curv0, conj)))
    step1 = spd_solve(curv1, norm1)
    keep = step0 + step1 + mm(conj, step1)
    coef = jnp.concatenate([keep.T, -mm(step0, step1).T], axis=1)
    return tuple(final_call(coef, innovation, info, back, cols, came))


def solution(mesh):
    one = P(("reg", "col"))
    in_specs = (P(None, ("reg", "col")), one, one, one, one, one, P(("reg", "col"), None), one, one)
    out_specs = (P(None, ("reg", "col")), P(None, ("reg", "col")))
    return jax.shard_map(
        on_device, mesh=mesh, in_specs=in_specs, out_specs=out_specs, check_vma=False
    )
```

```python
import functools

import jax
import jax.numpy as jnp
from jax import lax
from jax.experimental import pallas as pl
from jax.experimental.pallas import tpu as pltpu
from jax.sharding import PartitionSpec as P

ROWS = 1024
REACH = 2
COLS_DEV = 1024
META = 16
KB = 128
NB = 128
UNROLL = 4
SLOTS = (2 * REACH + 1) * (ROWS // KB) + 8
DEAD = 1e9
VMEM_LIMIT = 60 * 1024 * 1024

highest = lax.Precision.HIGHEST
f32 = jnp.float32
bf16 = jnp.bfloat16
NT = (((1,), (1,)), ((), ()))
NN = (((1,), (0,)), ((), ()))
TN = (((0,), (0,)), ((), ()))
vmem = pl.BlockSpec(memory_space=pltpu.VMEM)
smem = pl.BlockSpec(memory_space=pltpu.SMEM)


def shift(block, distance):
    axis = ("reg", "col")
    n = lax.axis_size(axis)
    return lax.ppermute(block, axis, [((i - distance) % n, i) for i in range(n)])


def dot(a, b, dims=NN):
    return lax.dot_general(a, b, dims, preferred_element_type=f32)


def two(x):
    hi = x.astype(bf16)
    return hi, (x - hi.astype(f32)).astype(bf16)


def three(x):
    hi = x.astype(bf16)
    rest = x - hi.astype(f32)
    mid = rest.astype(bf16)
    return hi, mid, (rest - mid.astype(f32)).astype(bf16)


def combine(coef_t, blocks):
    chi, clo = two(coef_t)
    bhi, blo = two(blocks)
    return dot(
        jnp.concatenate([chi, chi, clo], axis=1), jnp.concatenate([bhi, blo, bhi], axis=0)
    )


def params():
    return pltpu.CompilerParams(vmem_limit_bytes=VMEM_LIMIT)


def sort_kernel(innov_ref, meta_ref, out_ref, rank_ref):
    regions = innov_ref.shape[1] // ROWS

    def one(g, carry):
        cols = pl.ds(pl.multiple_of(g * ROWS, ROWS), ROWS)
        meta = meta_ref[:, cols]
        key = meta[6:7]
        live = (key < 0.5 * DEAD).astype(f32)
        key_col = jnp.broadcast_to(key, (128, ROWS)).T
        ranks = []
        sub = lax.broadcasted_iota(jnp.int32, (ROWS, 128), 0)
        lane = lax.broadcasted_iota(jnp.int32, (ROWS, 128), 1)
        for b in range(ROWS // 128):
            mine = key[:, b * 128 : (b + 1) * 128]
            before = (key_col < mine) | ((key_col == mine) & (sub < lane + b * 128))
            ranks.append(jnp.sum(before.astype(f32), axis=0, keepdims=True))
        rank = jnp.concatenate(ranks, axis=1)
        rank_ref[:, cols] = jnp.broadcast_to(rank, (8, ROWS))
        stack = jnp.concatenate([innov_ref[:, cols] * live, meta], axis=0)
        lhs = jnp.concatenate(three(stack), axis=0)
        n = stack.shape[0]
        rank_i = rank.astype(jnp.int32)
        for c in range(ROWS // 256):
            slot = lax.broadcasted_iota(jnp.int32, (256, ROWS), 0) + c * 256
            place = (slot == rank_i).astype(f32).astype(bf16)
            got = dot(lhs, place, NT)
            start = pl.multiple_of(g * ROWS + c * 256, 256)
            out_ref[:, pl.ds(start, 256)] = got[:n] + got[n : 2 * n] + got[2 * n :]
        return carry

    lax.fori_loop(0, regions, one, 0)


def sort_call(innov, meta):
    n = innov.shape[1]
    return pl.pallas_call(
        sort_kernel,
        out_shape=(
            jax.ShapeDtypeStruct((innov.shape[0] + META, n), f32),
            jax.ShapeDtypeStruct((8, n), f32),
        ),
        in_specs=[vmem, vmem],
        out_specs=(vmem, vmem),
        compiler_params=params(),
        name="sort_slots",
    )(innov, meta)


def build_list(bounds_ref, list_ref, count_ref, tiles):
    per = ROWS // NB

    def one(t, carry):
        g = t // per
        base = t * SLOTS

        def put(dh, jb, n):
            list_ref[base + n] = (g + dh) * (ROWS // KB) + jb
            return n + 1

        n = 0
        for dh in range(2 * REACH + 1):
            lo = bounds_ref[0, dh * tiles + t]
            hi = bounds_ref[1, dh * tiles + t]
            n = lax.fori_loop(lo, hi, functools.partial(put, dh), n)
        for p in range(UNROLL - 1):
            list_ref[base + n + p] = (tiles // per + 2 * REACH) * (ROWS // KB)
        count_ref[t] = n
        return carry

    lax.fori_loop(0, tiles, one, 0)


def apply_cov(list_ref, count_ref, row_ref, col_ref, v_ref, img_ref, stack_ref):
    ens, wide = v_ref.shape
    own = img_ref.shape[1]
    lead = REACH * ROWS
    tiles = own // NB
    chunk = 2048
    for c in range(wide // chunk):
        at = pl.ds(c * chunk, chunk)
        hi, lo = two(v_ref[:, at] * row_ref[2:3, at])
        stack_ref[0:ens, at] = hi
        stack_ref[ens : 2 * ens, at] = lo
    stack_ref[:, wide : wide + KB] = jnp.zeros((2 * ens, KB), bf16)

    def one(t, carry):
        i_at = pl.ds(pl.multiple_of(lead + t * NB, NB), NB)
        a_i = row_ref[0:1, i_at]
        b_i = row_ref[1:2, i_at]
        base = t * SLOTS

        def step(k, acc):
            his, los, vs = [], [], []
            for p in range(UNROLL):
                block = list_ref[base + k * UNROLL + p]
                j_at = pl.ds(pl.multiple_of(block * KB, KB), KB)
                da = col_ref[j_at, 0:1] - a_i
                db = col_ref[j_at, 1:2] - b_i
                r2 = da * da + db * db
                r = r2 * lax.rsqrt(jnp.maximum(r2, 1e-30))
                u = jnp.maximum(1.0 - r, 0.0)
                u2 = u * u
                shi, slo = two((u2 * u2) * (r + 0.25))
                his.append(shi)
                los.append(slo)
                vs.append(stack_ref[:, j_at])
            shi = jnp.concatenate(his, axis=0)
            slo = jnp.concatenate(los, axis=0)
            vs = jnp.concatenate(vs, axis=1)
            return (acc[0] + dot(vs, shi), acc[1] + dot(vs[:ens], slo))

        acc = (jnp.zeros((2 * ens, NB), f32), jnp.zeros((ens, NB), f32))
        trips = (count_ref[t] + UNROLL - 1) // UNROLL
        acc = lax.fori_loop(0, trips, step, acc)
        total = acc[0][:ens] + acc[0][ens:] + acc[1]
        o_at = pl.ds(pl.multiple_of(t * NB, NB), NB)
        img_ref[:, o_at] = total * (row_ref[2:3, i_at] * 0.25) + row_ref[3:4, i_at] * v_ref[:, i_at]
        return carry

    lax.fori_loop(0, tiles, one, 0)


def gram(a, b):
    return lax.dot_general(a, b, NT, precision=highest, preferred_element_type=f32)


def first_kernel(
    bounds_ref, row_ref, col_ref, v_ref, img_ref, gram_ref, list_ref, count_ref, stack_ref
):
    own = img_ref.shape[1]
    lead = REACH * ROWS
    build_list(bounds_ref, list_ref, count_ref, own // NB)
    apply_cov(list_ref, count_ref, row_ref, col_ref, v_ref, img_ref, stack_ref)
    r = v_ref[:, lead : lead + own]
    gram_ref[...] = gram(r, jnp.concatenate([r, img_ref[...]], axis=0))


def second_kernel(
    list_ref,
    count_ref,
    row_ref,
    col_ref,
    step_ref,
    r0_ref,
    img0_ref,
    gram_ref,
    img_ref,
    v_ref,
    stack_ref,
):
    ens, own = img_ref.shape
    lead = REACH * ROWS
    chunk = 2048
    step_t = step_ref[...].T
    for c in range(v_ref.shape[1] // chunk):
        at = pl.ds(c * chunk, chunk)
        v_ref[:, at] = r0_ref[:, at] - combine(step_t, img0_ref[:, at])
    apply_cov(list_ref, count_ref, row_ref, col_ref, v_ref, img_ref, stack_ref)
    r = v_ref[:, lead : lead + own]
    gram_ref[:ens] = gram(r, jnp.concatenate([r, img_ref[...]], axis=0))
    mixed = gram(r, img0_ref[:, lead : lead + own])
    gram_ref[ens:] = jnp.concatenate([mixed, mixed], axis=1)


def first_call(bounds, row, col, v, own):
    ens, wide = v.shape
    tiles = own // NB
    return pl.pallas_call(
        first_kernel,
        out_shape=(
            jax.ShapeDtypeStruct((ens, own), f32),
            jax.ShapeDtypeStruct((ens, 2 * ens), f32),
            jax.ShapeDtypeStruct((tiles * SLOTS,), jnp.int32),
            jax.ShapeDtypeStruct((tiles,), jnp.int32),
        ),
        in_specs=[smem, vmem, vmem, vmem],
        out_specs=(vmem, vmem, smem, smem),
        scratch_shapes=[pltpu.VMEM((2 * ens, wide + KB), bf16)],
        compiler_params=params(),
        name="operate_first",
    )(bounds, row, col, v)


def second_call(blocks, counts, row, col, step, r0, img0, own):
    ens, wide = r0.shape
    return pl.pallas_call(
        second_kernel,
        out_shape=jax.ShapeDtypeStruct((2 * ens, 2 * ens), f32),
        in_specs=[smem, smem, vmem, vmem, vmem, vmem, vmem],
        out_specs=vmem,
        scratch_shapes=[
            pltpu.VMEM((ens, own), f32),
            pltpu.VMEM((ens, wide), f32),
            pltpu.VMEM((2 * ens, wide + KB), bf16),
        ],
        compiler_params=params(),
        name="operate_second",
    )(blocks, counts, row, col, step, r0, img0)


def reduce_kernel(steps, n_col, x_ref, out_ref, send, recv, send_sem, recv_sem):
    me = lax.axis_index("reg") * n_col + lax.axis_index("col")
    partners = []
    for k in range(steps):
        size = 2**k
        other = me + size * (1 - 2 * ((me // size) % 2))
        partners.append((other // n_col, other % n_col))
    barrier = pltpu.get_barrier_semaphore()
    for other in partners:
        pl.semaphore_signal(
            barrier, inc=1, device_id=other, device_id_type=pl.DeviceIdType.MESH
        )
    pl.semaphore_wait(barrier, steps)
    total = x_ref[...]
    for k in range(steps):
        if k:
            send[k] = total
        copy = pltpu.make_async_remote_copy(
            src_ref=send.at[k] if k else x_ref,
            dst_ref=recv.at[k],
            send_sem=send_sem.at[k],
            recv_sem=recv_sem.at[k],
            device_id=partners[k],
            device_id_type=pl.DeviceIdType.MESH,
        )
        copy.start()
        copy.wait()
        total = total + recv[k]
    out_ref[...] = total


def sum_all(x, which):
    n_col = lax.axis_size("col")
    steps = (lax.axis_size("reg") * n_col).bit_length() - 1
    return pl.pallas_call(
        functools.partial(reduce_kernel, steps, n_col),
        out_shape=jax.ShapeDtypeStruct(x.shape, f32),
        in_specs=[vmem],
        out_specs=vmem,
        scratch_shapes=[
            pltpu.VMEM((steps,) + x.shape, f32),
            pltpu.VMEM((steps,) + x.shape, f32),
            pltpu.SemaphoreType.DMA((steps,)),
            pltpu.SemaphoreType.DMA((steps,)),
        ],
        compiler_params=pltpu.CompilerParams(collective_id=which, has_side_effects=True),
        name="sum_all",
    )(x)


def symmetric(matrix):
    return 0.5 * (matrix + matrix.T)


def mm(a, b, dims=NN):
    return lax.dot_general(a, b, dims, precision=highest, preferred_element_type=f32)


def eliminate(chains):
    ens, both = chains[0].shape
    rows = lax.broadcasted_iota(jnp.int32, (ens, both), 0)
    for k in range(ens):
        done = []
        for m in chains:
            col = jnp.broadcast_to(m[:, k : k + 1], (ens, both))
            pivot = m[k : k + 1] / col[k : k + 1]
            done.append(jnp.where(rows == k, pivot, m - col * pivot))
        chains = done
    return [m[:, ens:] for m in chains]


def solve_first_kernel(gram_ref, step_ref, inv_ref, curv_ref):
    ens = gram_ref.shape[0]
    norm = symmetric(gram_ref[:, :ens])
    curv = symmetric(gram_ref[:, ens:])
    rows = lax.broadcasted_iota(jnp.int32, (ens, ens), 0)
    eye = (rows == lax.broadcasted_iota(jnp.int32, (ens, ens), 1)).astype(f32)
    step, inv = eliminate(
        [jnp.concatenate([curv, norm], axis=1), jnp.concatenate([norm, eye], axis=1)]
    )
    step_ref[...] = step
    inv_ref[...] = inv
    curv_ref[...] = curv


def solve_second_kernel(gram_ref, step_ref, inv_ref, curv_ref, coef_ref):
    ens = step_ref.shape[0]
    norm = symmetric(gram_ref[:ens, :ens])
    cross = gram_ref[:ens, ens:]
    mixed = gram_ref[ens:, :ens]
    conj = mm(inv_ref[...], norm)
    coupled = mm(mixed, conj)
    quad = mm(conj, mm(curv_ref[...], conj), TN)
    curv = symmetric(cross + coupled + coupled.T + quad)
    (step,) = eliminate([jnp.concatenate([curv, norm], axis=1)])
    step0 = step_ref[...]
    keep = step0 + step + mm(conj, step)
    coef_ref[...] = jnp.concatenate([keep.T, -mm(step0, step).T], axis=1)


def solve_first(grams):
    ens = grams.shape[0]
    small = jax.ShapeDtypeStruct((ens, ens), f32)
    return pl.pallas_call(
        solve_first_kernel,
        out_shape=(small, small, small),
        in_specs=[vmem],
        out_specs=(vmem, vmem, vmem),
        name="solve_first",
    )(grams)


def solve_second(grams, step0, inv0, curv0):
    ens = step0.shape[0]
    return pl.pallas_call(
        solve_second_kernel,
        out_shape=jax.ShapeDtypeStruct((ens, 2 * ens), f32),
        in_specs=[vmem] * 4,
        out_specs=vmem,
        name="solve_second",
    )(grams, step0, inv0, curv0)


def columns_kernel(innov_ref, info_ref, rank_ref, img_ref, back_ref, cols_ref):
    ens, own = innov_ref.shape
    regions = own // ROWS
    cols_ref[...] = jnp.zeros_like(cols_ref)

    def one(g, carry):
        at = pl.ds(pl.multiple_of(g * ROWS, ROWS), ROWS)
        rank = rank_ref[0:1, at].astype(jnp.int32)
        lhs = jnp.concatenate(two(img_ref[:, at]), axis=0)
        total = jnp.zeros((2 * ens, ROWS), f32)
        for c in range(ROWS // 256):
            slot = lax.broadcasted_iota(jnp.int32, (256, ROWS), 0) + c * 256
            place = (slot == rank).astype(f32).astype(bf16)
            total = total + dot(lhs[:, c * 256 : (c + 1) * 256], place)
        image = total[:ens] + total[ens:]
        back_ref[:, at] = image
        gain = info_ref[0:1, at]
        live = info_ref[1:2, at]
        owner = info_ref[2:3, at].astype(jnp.int32)
        rhi, rlo = two(innov_ref[:, at] * (gain * live))
        ihi, ilo = two(image * gain)
        stack = jnp.concatenate([rhi, ihi, rlo, ilo], axis=0)
        for c in range(2 * COLS_DEV // 256):
            slot = lax.broadcasted_iota(jnp.int32, (256, ROWS), 0) + c * 256
            hot = (slot == owner).astype(f32).astype(bf16)
            got = dot(stack, hot, NT)
            part = pl.ds(c * 256, 256)
            cols_ref[:, part] += got[: 2 * ens] + got[2 * ens :]
        return carry

    lax.fori_loop(0, regions, one, 0)


def columns_call(innov, info, rank, img):
    ens, own = innov.shape
    return pl.pallas_call(
        columns_kernel,
        out_shape=(
            jax.ShapeDtypeStruct((ens, own), f32),
            jax.ShapeDtypeStruct((2 * ens, 2 * COLS_DEV), f32),
        ),
        in_specs=[vmem] * 4,
        out_specs=(vmem, vmem),
        compiler_params=params(),
        cost_estimate=pl.CostEstimate(
            flops=2 * 256 * own * 3072, bytes_accessed=4 << 20, transcendentals=0
        ),
        name="columns",
    )(innov, info, rank, img)


def final_kernel(coef_ref, innov_ref, info_ref, back_ref, cols_ref, came_ref, w_ref, inc_ref):
    coef = coef_ref[...]
    ens = coef.shape[0]
    own = innov_ref.shape[1]
    chunk = 1024
    first, second = coef[:, :ens], coef[:, ens:]
    for c in range(own // chunk):
        at = pl.ds(c * chunk, chunk)
        live = info_ref[1:2, at]
        w_ref[:, at] = combine(first, innov_ref[:, at] * live) + combine(second, back_ref[:, at])
    both = cols_ref[:, :COLS_DEV] + came_ref[...]
    inc_ref[...] = combine(first, both[:ens]) + combine(second, both[ens:])


def final_call(coef, innov, info, back, cols, came):
    ens, own = innov.shape
    return pl.pallas_call(
        final_kernel,
        out_shape=(
            jax.ShapeDtypeStruct((ens, own), f32),
            jax.ShapeDtypeStruct((ens, COLS_DEV), f32),
        ),
        in_specs=[vmem] * 6,
        out_specs=(vmem, vmem),
        compiler_params=params(),
        name="final",
    )(coef, innov, info, back, cols, came)


def block_bounds(key_ext, flags_ext, regions):
    wide = regions + 2 * REACH
    jkeys = key_ext.reshape(wide, ROWS // KB, KB)
    jmin = jkeys.min(axis=2)
    jmax = jnp.where(jkeys < 0.5 * DEAD, jkeys, -DEAD).max(axis=2)
    ikeys = key_ext.reshape(wide, ROWS // NB, NB)[REACH : REACH + regions]
    imin = ikeys.min(axis=2)
    imax = jnp.where(ikeys < 0.5 * DEAD, ikeys, -DEAD).max(axis=2)
    los, his = [], []
    ids = jnp.arange(ROWS // KB, dtype=jnp.int32)[None, None, :]
    for dh in range(2 * REACH + 1):
        lo_j = jmin[dh : dh + regions]
        hi_j = jmax[dh : dh + regions]
        d = dh - REACH
        if d == 0:
            flag = jnp.ones((regions,), jnp.bool_)
        elif d > 0:
            flag = flags_ext[d - 1, REACH : REACH + regions] > 0.5
        else:
            flag = flags_ext[-d - 1, REACH + d : REACH + d + regions] > 0.5
        near = (
            (hi_j[:, None, :] >= imin[:, :, None] - 1.001)
            & (lo_j[:, None, :] <= imax[:, :, None] + 1.001)
            & (imin[:, :, None] < 0.5 * DEAD)
            & flag[:, None, None]
        )
        los.append(jnp.where(near, ids, ROWS // KB).min(axis=2).reshape(-1))
        his.append(jnp.where(near, ids + 1, 0).max(axis=2).reshape(-1))
    return jnp.stack([jnp.concatenate(los), jnp.concatenate(his)])


def on_device(
    innovation,
    obs_along,
    obs_across,
    obs_scale,
    obs_error,
    obs_gain,
    pair_live,
    obs_count,
    col_owner,
):
    axes = ("reg", "col")
    regions = obs_count.shape[0]
    ens, own = innovation.shape
    halo = REACH * ROWS
    live = (
        (jnp.arange(ROWS, dtype=jnp.int32)[None, :] < obs_count[:, None])
        .astype(f32)
        .reshape(own)
    )
    flags = jnp.repeat(pair_live.astype(f32).T, ROWS, axis=1)
    zero = jnp.zeros((own,), f32)
    meta = jnp.stack(
        [obs_along, obs_across, obs_scale * live, obs_error, flags[0], flags[1]]
        + [jnp.where(live > 0.5, obs_across, DEAD)]
        + [zero] * (META - 7)
    )
    total_cols = COLS_DEV * lax.axis_size(axes)
    local_col = (col_owner - lax.axis_index(axes) * COLS_DEV) % total_cols
    info = jnp.stack([obs_gain, live, local_col.astype(f32)] + [zero] * 5)

    ordered, rank = sort_call(innovation, meta)
    after = shift(ordered[:, :halo], -1)
    before = shift(ordered[:, own - halo :], 1)
    ext = jnp.concatenate([before, ordered, after], axis=1)
    r0 = ext[:ens]
    region_ids = jnp.repeat(jnp.arange(regions + 2 * REACH, dtype=f32), ROWS)
    row = ext[ens : ens + 8]
    row = row.at[0].add(region_ids)
    col = jnp.pad(row, ((0, 0), (0, KB))).T
    bounds = block_bounds(row[6], row[4:6, ::ROWS], regions)

    img0, grams, blocks, counts = first_call(bounds, row, col, r0, own)
    img_after = shift(img0[:, :halo], -1)
    img_before = shift(img0[:, own - halo :], 1)
    step0, inv0, curv0 = solve_first(sum_all(grams, 0))
    img_ext = jnp.concatenate([img_before, img0, img_after], axis=1)
    back, cols = columns_call(innovation, info, rank, img0)
    came = shift(cols[:, COLS_DEV:], 1)
    grams = second_call(blocks, counts, row, col, step0, r0, img_ext, own)
    coef = solve_second(sum_all(grams, 1), step0, inv0, curv0)
    return tuple(final_call(coef, innovation, info, back, cols, came))


def solution(mesh):
    one = P(("reg", "col"))
    in_specs = (P(None, ("reg", "col")), one, one, one, one, one, P(("reg", "col"), None), one, one)
    out_specs = (P(None, ("reg", "col")), P(None, ("reg", "col")))
    return jax.shard_map(
        on_device, mesh=mesh, in_specs=in_specs, out_specs=out_specs, check_vma=False
    )
```

```python
import functools

import jax
import jax.numpy as jnp
from jax import lax
from jax.experimental import pallas as pl
from jax.experimental.pallas import tpu as pltpu
from jax.sharding import PartitionSpec as P

ROWS = 1024
REACH = 2
COLS_DEV = 1024
META = 16
KB = 128
NB = 128
UNROLL = 4
DEAD = 1e9
VMEM_LIMIT = 60 * 1024 * 1024

highest = lax.Precision.HIGHEST
f32 = jnp.float32
bf16 = jnp.bfloat16
NT = (((1,), (1,)), ((), ()))
NN = (((1,), (0,)), ((), ()))
TN = (((0,), (0,)), ((), ()))
vmem = pl.BlockSpec(memory_space=pltpu.VMEM)
smem = pl.BlockSpec(memory_space=pltpu.SMEM)


def shift(block, distance):
    axis = ("reg", "col")
    n = lax.axis_size(axis)
    return lax.ppermute(block, axis, [((i - distance) % n, i) for i in range(n)])


def dot(a, b, dims=NN):
    return lax.dot_general(a, b, dims, preferred_element_type=f32)


def two(x):
    hi = x.astype(bf16)
    return hi, (x - hi.astype(f32)).astype(bf16)


def three(x):
    hi = x.astype(bf16)
    rest = x - hi.astype(f32)
    mid = rest.astype(bf16)
    return hi, mid, (rest - mid.astype(f32)).astype(bf16)


def combine(coef_t, blocks):
    chi, clo = two(coef_t)
    bhi, blo = two(blocks)
    return dot(
        jnp.concatenate([chi, chi, clo], axis=1), jnp.concatenate([bhi, blo, bhi], axis=0)
    )


def params():
    return pltpu.CompilerParams(vmem_limit_bytes=VMEM_LIMIT)


def sort_kernel(innov_ref, meta_ref, first_ref, last_ref, rank_ref):
    regions = innov_ref.shape[1] // ROWS
    kept = first_ref.shape[0]
    sub = lax.broadcasted_iota(jnp.int32, (ROWS, 128), 0)
    lane = lax.broadcasted_iota(jnp.int32, (ROWS, 128), 1)
    for g in range(regions):
        cols = pl.ds(g * ROWS, ROWS)
        meta = meta_ref[:, cols]
        key = meta[6:7]
        live = (key < 0.5 * DEAD).astype(f32)
        key_col = jnp.broadcast_to(key, (128, ROWS)).T
        ranks = []
        for b in range(ROWS // 128):
            mine = key[:, b * 128 : (b + 1) * 128]
            before = (key_col < mine) | ((key_col == mine) & (sub < lane + b * 128))
            ranks.append(jnp.sum(before.astype(f32), axis=0, keepdims=True))
        rank = jnp.concatenate(ranks, axis=1)
        rank_ref[:, cols] = jnp.broadcast_to(rank, (8, ROWS))
        stack = jnp.concatenate([innov_ref[:, cols] * live, meta], axis=0)
        lhs = jnp.concatenate(three(stack), axis=0)
        n = stack.shape[0]
        rank_i = rank.astype(jnp.int32)
        out_ref = first_ref if g < regions // 2 else last_ref
        for c in range(ROWS // 256):
            slot = lax.broadcasted_iota(jnp.int32, (256, ROWS), 0) + c * 256
            place = (slot == rank_i).astype(f32).astype(bf16)
            got = dot(lhs, place, NT)
            start = (g % (regions // 2)) * ROWS + c * 256
            out_ref[:, start : start + 256] = (got[:n] + got[n : 2 * n] + got[2 * n :])[:kept]


def sort_call(innov, meta):
    ens, n = innov.shape
    half = jax.ShapeDtypeStruct((ens + 8, n // 2), f32)
    return pl.pallas_call(
        sort_kernel,
        out_shape=(half, half, jax.ShapeDtypeStruct((8, n), f32)),
        in_specs=[vmem, vmem],
        out_specs=(vmem, vmem, vmem),
        compiler_params=params(),
        name="sort_slots",
    )(innov, meta)


def build_list(bounds_ref, list_ref, tile_ref, count_ref, tiles):
    per = ROWS // NB
    zero_block = (tiles // per + 2 * REACH) * (ROWS // KB)

    def one(t, trip):
        g = t // per
        base = trip * UNROLL

        def put(dh, jb, n):
            list_ref[n] = (g + dh) * (ROWS // KB) + jb
            return n + 1

        n = base
        for dh in range(2 * REACH + 1):
            lo = bounds_ref[0, dh * tiles + t]
            hi = bounds_ref[1, dh * tiles + t]
            n = lax.fori_loop(lo, hi, functools.partial(put, dh), n)
        for p in range(UNROLL):
            list_ref[n + p] = zero_block
        end = (n + UNROLL - 1) // UNROLL

        def mark(k, carry):
            tile_ref[k] = t
            return carry

        lax.fori_loop(trip, end, mark, 0)
        return end

    trips = lax.fori_loop(0, tiles, one, 0)
    tile_ref[trips] = 0
    for p in range(UNROLL):
        list_ref[trips * UNROLL + p] = zero_block
    count_ref[0] = trips


def prepare(chunks, row_ref, along_ref, across_ref):
    width = chunks[0].shape[1]
    per = width // ROWS
    for c, ref in enumerate(chunks):
        row_ref[:, c * width : (c + 1) * width] = ref[ref.shape[0] - 8 :, :]
        for r in range(per):
            h = c * per + r
            at = slice(h * ROWS, (h + 1) * ROWS)
            row_ref[0:1, at] = row_ref[0:1, at] + float(h)
            col = row_ref[:, at].T
            along_ref[at, :] = jnp.broadcast_to(col[:, 0:1], (ROWS, NB))
            across_ref[at, :] = jnp.broadcast_to(col[:, 1:2], (ROWS, NB))
    wide = width * len(chunks)
    along_ref[wide : wide + KB, :] = jnp.zeros((KB, NB), f32)
    across_ref[wide : wide + KB, :] = jnp.zeros((KB, NB), f32)


def apply_cov(list_ref, tile_ref, count_ref, row_ref, along_ref, across_ref, v_ref, img_ref, stack_ref, s_ref):
    ens, wide = v_ref.shape
    own = img_ref.shape[1]
    lead = REACH * ROWS
    chunk = 2048
    for c in range(wide // chunk):
        at = pl.ds(c * chunk, chunk)
        hi, lo = two(v_ref[:, at] * row_ref[2:3, at])
        stack_ref[0:ens, at] = hi
        stack_ref[ens : 2 * ens, at] = lo
    stack_ref[:, wide : wide + KB] = jnp.zeros((2 * ens, KB), bf16)
    s_ref[...] = jnp.zeros_like(s_ref)
    img_ref[...] = jnp.zeros_like(img_ref)
    depth = UNROLL * KB

    def step(k, carry):
        before = jnp.maximum(k - 1, 0)
        vhi, vlo = [], []
        for p in range(UNROLL):
            block = list_ref[before * UNROLL + p]
            part = stack_ref[:, pl.ds(pl.multiple_of(block * KB, KB), KB)]
            vhi.append(part[:ens])
            vlo.append(part[ens:])
        lhs = jnp.concatenate(vhi + vlo + vhi, axis=1)
        shi = s_ref[:depth]
        rhs = jnp.concatenate([shi, shi, s_ref[depth:]], axis=0)
        o_at = pl.ds(pl.multiple_of(tile_ref[before] * NB, NB), NB)
        img_ref[:, o_at] += dot(lhs, rhs)
        i_at = pl.ds(pl.multiple_of(lead + tile_ref[k] * NB, NB), NB)
        a_i = row_ref[0:1, i_at]
        b_i = row_ref[1:2, i_at]
        for p in range(UNROLL):
            block = list_ref[k * UNROLL + p]
            j_at = pl.ds(pl.multiple_of(block * KB, KB), KB)
            da = along_ref[j_at, :] - a_i
            db = across_ref[j_at, :] - b_i
            r2 = da * da + db * db
            r = r2 * lax.rsqrt(jnp.maximum(r2, 1e-30))
            u = jnp.maximum(1.0 - r, 0.0)
            u2 = u * u
            hi, lo = two((u2 * u2) * (r + 0.25))
            s_ref[p * KB : (p + 1) * KB] = hi
            s_ref[depth + p * KB : depth + (p + 1) * KB] = lo
        return carry

    lax.fori_loop(0, count_ref[0] + 1, step, 0)
    for c in range(own // chunk):
        at = slice(c * chunk, (c + 1) * chunk)
        e_at = slice(lead + c * chunk, lead + (c + 1) * chunk)
        img_ref[:, at] = (
            img_ref[:, at] * (row_ref[2:3, e_at] * 0.25) + row_ref[3:4, e_at] * v_ref[:, e_at]
        )


def gram(a, b):
    ahi, alo = two(a)
    bhi, blo = two(b)
    return dot(
        jnp.concatenate([ahi, ahi, alo], axis=1), jnp.concatenate([bhi, blo, bhi], axis=1), NT
    )


def first_kernel(
    bounds_ref,
    c0,
    c1,
    c2,
    c3,
    imga_ref,
    imgb_ref,
    gram_ref,
    list_ref,
    tile_ref,
    count_ref,
    row_ref,
    along_ref,
    across_ref,
    v_ref,
    img_ref,
    stack_ref,
    s_ref,
):
    ens, own = img_ref.shape
    lead = REACH * ROWS
    chunks = [c0, c1, c2, c3]
    build_list(bounds_ref, list_ref, tile_ref, count_ref, own // NB)
    prepare(chunks, row_ref, along_ref, across_ref)
    for c, ref in enumerate(chunks):
        v_ref[:, c * lead : (c + 1) * lead] = ref[:ens, :]
    apply_cov(
        list_ref, tile_ref, count_ref, row_ref, along_ref, across_ref, v_ref, img_ref, stack_ref, s_ref
    )
    imga_ref[...] = img_ref[:, :lead]
    imgb_ref[...] = img_ref[:, lead:]
    r = v_ref[:, lead : lead + own]
    gram_ref[...] = gram(r, jnp.concatenate([r, img_ref[...]], axis=0))


def second_kernel(
    list_ref,
    tile_ref,
    count_ref,
    step_ref,
    c0,
    c1,
    c2,
    c3,
    i0,
    i1,
    i2,
    i3,
    gram_ref,
    row_ref,
    along_ref,
    across_ref,
    v_ref,
    img_ref,
    stack_ref,
    s_ref,
):
    ens, own = img_ref.shape
    lead = REACH * ROWS
    chunks = [c0, c1, c2, c3]
    prepare(chunks, row_ref, along_ref, across_ref)
    step_t = step_ref[...].T
    for c, (ref, image) in enumerate(zip(chunks, [i0, i1, i2, i3])):
        v_ref[:, c * lead : (c + 1) * lead] = ref[:ens, :] - combine(step_t, image[...])
    apply_cov(
        list_ref, tile_ref, count_ref, row_ref, along_ref, across_ref, v_ref, img_ref, stack_ref, s_ref
    )
    r = v_ref[:, lead : lead + own]
    gram_ref[:ens] = gram(r, jnp.concatenate([r, img_ref[...]], axis=0))
    mixed = gram(r, jnp.concatenate([i1[...], i2[...]], axis=1))
    gram_ref[ens:] = jnp.concatenate([mixed, mixed], axis=1)


def scratch(ens, own):
    wide = own + 2 * REACH * ROWS
    return [
        pltpu.VMEM((8, wide), f32),
        pltpu.VMEM((wide + KB, NB), f32),
        pltpu.VMEM((wide + KB, NB), f32),
        pltpu.VMEM((ens, wide), f32),
        pltpu.VMEM((ens, own), f32),
        pltpu.VMEM((2 * ens, wide + KB), bf16),
        pltpu.VMEM((2 * UNROLL * KB, NB), bf16),
    ]


def first_call(bounds, chunks, ens, own):
    tiles = own // NB
    trips = tiles * -(-(2 * REACH + 1) * (ROWS // KB) // UNROLL) + 2
    half = jax.ShapeDtypeStruct((ens, own // 2), f32)
    return pl.pallas_call(
        first_kernel,
        out_shape=(
            half,
            half,
            jax.ShapeDtypeStruct((ens, 2 * ens), f32),
            jax.ShapeDtypeStruct((trips * UNROLL,), jnp.int32),
            jax.ShapeDtypeStruct((trips,), jnp.int32),
            jax.ShapeDtypeStruct((1,), jnp.int32),
        ),
        in_specs=[smem] + [vmem] * 4,
        out_specs=(vmem, vmem, vmem, smem, smem, smem),
        scratch_shapes=scratch(ens, own),
        compiler_params=params(),
        name="operate_first",
    )(bounds, *chunks)


def second_call(lists, step, chunks, images, ens, own):
    return pl.pallas_call(
        second_kernel,
        out_shape=jax.ShapeDtypeStruct((2 * ens, 2 * ens), f32),
        in_specs=[smem] * 3 + [vmem] * 9,
        out_specs=vmem,
        scratch_shapes=scratch(ens, own),
        compiler_params=params(),
        name="operate_second",
    )(*lists, step, *chunks, *images)


def reduce_kernel(steps, n_col, x_ref, out_ref, send, recv, send_sem, recv_sem):
    me = lax.axis_index("reg") * n_col + lax.axis_index("col")
    partners = []
    for k in range(steps):
        size = 2**k
        other = me + size * (1 - 2 * ((me // size) % 2))
        partners.append((other // n_col, other % n_col))
    barrier = pltpu.get_barrier_semaphore()
    for other in partners:
        pl.semaphore_signal(
            barrier, inc=1, device_id=other, device_id_type=pl.DeviceIdType.MESH
        )
    pl.semaphore_wait(barrier, steps)
    total = x_ref[...]
    for k in range(steps):
        if k:
            send[k] = total
        copy = pltpu.make_async_remote_copy(
            src_ref=send.at[k] if k else x_ref,
            dst_ref=recv.at[k],
            send_sem=send_sem.at[k],
            recv_sem=recv_sem.at[k],
            device_id=partners[k],
            device_id_type=pl.DeviceIdType.MESH,
        )
        copy.start()
        copy.wait()
        total = total + recv[k]
    out_ref[...] = total


def sum_all(x, which):
    n_col = lax.axis_size("col")
    steps = (lax.axis_size("reg") * n_col).bit_length() - 1
    return pl.pallas_call(
        functools.partial(reduce_kernel, steps, n_col),
        out_shape=jax.ShapeDtypeStruct(x.shape, f32),
        in_specs=[vmem],
        out_specs=vmem,
        scratch_shapes=[
            pltpu.VMEM((steps,) + x.shape, f32),
            pltpu.VMEM((steps,) + x.shape, f32),
            pltpu.SemaphoreType.DMA((steps,)),
            pltpu.SemaphoreType.DMA((steps,)),
        ],
        compiler_params=pltpu.CompilerParams(collective_id=which, has_side_effects=True),
        name="sum_all",
    )(x)


def symmetric(matrix):
    return 0.5 * (matrix + matrix.T)


def mm(a, b, dims=NN):
    return lax.dot_general(a, b, dims, precision=highest, preferred_element_type=f32)


def eliminate(chains):
    ens, both = chains[0].shape
    rows = lax.broadcasted_iota(jnp.int32, (ens, both), 0)
    for k in range(ens):
        done = []
        for m in chains:
            col = jnp.broadcast_to(m[:, k : k + 1], (ens, both))
            pivot = m[k : k + 1] / col[k : k + 1]
            done.append(jnp.where(rows == k, pivot, m - col * pivot))
        chains = done
    return [m[:, ens:] for m in chains]


def solve_first_kernel(gram_ref, step_ref, inv_ref, curv_ref):
    ens = gram_ref.shape[0]
    norm = symmetric(gram_ref[:, :ens])
    curv = symmetric(gram_ref[:, ens:])
    rows = lax.broadcasted_iota(jnp.int32, (ens, ens), 0)
    eye = (rows == lax.broadcasted_iota(jnp.int32, (ens, ens), 1)).astype(f32)
    step, inv = eliminate(
        [jnp.concatenate([curv, norm], axis=1), jnp.concatenate([norm, eye], axis=1)]
    )
    step_ref[...] = step
    inv_ref[...] = inv
    curv_ref[...] = curv


def solve_second_kernel(gram_ref, step_ref, inv_ref, curv_ref, coef_ref):
    ens = step_ref.shape[0]
    norm = symmetric(gram_ref[:ens, :ens])
    cross = gram_ref[:ens, ens:]
    mixed = gram_ref[ens:, :ens]
    conj = mm(inv_ref[...], norm)
    coupled = mm(mixed, conj)
    quad = mm(conj, mm(curv_ref[...], conj), TN)
    curv = symmetric(cross + coupled + coupled.T + quad)
    (step,) = eliminate([jnp.concatenate([curv, norm], axis=1)])
    step0 = step_ref[...]
    keep = step0 + step + mm(conj, step)
    coef_ref[...] = jnp.concatenate([keep.T, -mm(step0, step).T], axis=1)


def solve_first(grams):
    ens = grams.shape[0]
    small = jax.ShapeDtypeStruct((ens, ens), f32)
    return pl.pallas_call(
        solve_first_kernel,
        out_shape=(small, small, small),
        in_specs=[vmem],
        out_specs=(vmem, vmem, vmem),
        name="solve_first",
    )(grams)


def solve_second(grams, step0, inv0, curv0):
    ens = step0.shape[0]
    return pl.pallas_call(
        solve_second_kernel,
        out_shape=jax.ShapeDtypeStruct((ens, 2 * ens), f32),
        in_specs=[vmem] * 4,
        out_specs=vmem,
        name="solve_second",
    )(grams, step0, inv0, curv0)


def add_columns(stack, owner, cols_ref):
    ens = cols_ref.shape[0]
    for c in range(2 * COLS_DEV // 256):
        slot = lax.broadcasted_iota(jnp.int32, (256, ROWS), 0) + c * 256
        hot = (slot == owner).astype(f32).astype(bf16)
        got = dot(stack, hot, NT)
        part = slice(c * 256, (c + 1) * 256)
        cols_ref[:, part] += got[:ens] + got[ens:]


def innov_columns_kernel(innov_ref, info_ref, cols_ref):
    cols_ref[...] = jnp.zeros_like(cols_ref)

    def one(g, carry):
        at = pl.ds(pl.multiple_of(g * ROWS, ROWS), ROWS)
        scale = info_ref[0:1, at] * info_ref[1:2, at]
        owner = info_ref[2:3, at].astype(jnp.int32)
        add_columns(jnp.concatenate(two(innov_ref[:, at] * scale), axis=0), owner, cols_ref)
        return carry

    lax.fori_loop(0, innov_ref.shape[1] // ROWS, one, 0)


def columns_kernel(info_ref, rank_ref, imga_ref, imgb_ref, back_ref, cols_ref):
    ens, own = back_ref.shape
    half = own // 2
    cols_ref[...] = jnp.zeros_like(cols_ref)
    for g in range(own // ROWS):
        at = slice(g * ROWS, (g + 1) * ROWS)
        rank = rank_ref[0:1, at].astype(jnp.int32)
        img_ref = imga_ref if g * ROWS < half else imgb_ref
        begin = (g * ROWS) % half
        lhs = jnp.concatenate(two(img_ref[:, begin : begin + ROWS]), axis=0)
        total = jnp.zeros((2 * ens, ROWS), f32)
        for c in range(ROWS // 256):
            slot = lax.broadcasted_iota(jnp.int32, (256, ROWS), 0) + c * 256
            place = (slot == rank).astype(f32).astype(bf16)
            total = total + dot(lhs[:, c * 256 : (c + 1) * 256], place)
        image = total[:ens] + total[ens:]
        back_ref[:, at] = image
        owner = info_ref[2:3, at].astype(jnp.int32)
        add_columns(jnp.concatenate(two(image * info_ref[0:1, at]), axis=0), owner, cols_ref)


def innov_columns_call(innov, info):
    ens, own = innov.shape
    return pl.pallas_call(
        innov_columns_kernel,
        out_shape=jax.ShapeDtypeStruct((ens, 2 * COLS_DEV), f32),
        in_specs=[vmem] * 2,
        out_specs=vmem,
        compiler_params=params(),
        cost_estimate=pl.CostEstimate(
            flops=2 * 256 * own * 2048, bytes_accessed=4 << 20, transcendentals=0
        ),
        name="innov_columns",
    )(innov, info)


def columns_call(info, rank, imga, imgb):
    ens, half = imga.shape
    return pl.pallas_call(
        columns_kernel,
        out_shape=(
            jax.ShapeDtypeStruct((ens, 2 * half), f32),
            jax.ShapeDtypeStruct((ens, 2 * COLS_DEV), f32),
        ),
        in_specs=[vmem] * 4,
        out_specs=(vmem, vmem),
        compiler_params=params(),
        cost_estimate=pl.CostEstimate(
            flops=2 * 256 * 2 * half * 3072, bytes_accessed=4 << 20, transcendentals=0
        ),
        name="columns",
    )(info, rank, imga, imgb)


def final_kernel(coef_ref, innov_ref, info_ref, back_ref, rc_ref, rin_ref, ic_ref, iin_ref, w_ref, inc_ref):
    coef = coef_ref[...]
    ens = coef.shape[0]
    own = innov_ref.shape[1]
    chunk = 1024
    first, second = coef[:, :ens], coef[:, ens:]
    for c in range(own // chunk):
        at = pl.ds(c * chunk, chunk)
        live = info_ref[1:2, at]
        w_ref[:, at] = combine(first, innov_ref[:, at] * live) + combine(second, back_ref[:, at])
    inc_ref[...] = combine(first, rc_ref[:, :COLS_DEV] + rin_ref[...]) + combine(
        second, ic_ref[:, :COLS_DEV] + iin_ref[...]
    )


def final_call(coef, innov, info, back, *cols):
    ens, own = innov.shape
    return pl.pallas_call(
        final_kernel,
        out_shape=(
            jax.ShapeDtypeStruct((ens, own), f32),
            jax.ShapeDtypeStruct((ens, COLS_DEV), f32),
        ),
        in_specs=[vmem] * 8,
        out_specs=(vmem, vmem),
        compiler_params=params(),
        name="final",
    )(coef, innov, info, back, *cols)


def block_bounds(key_ext, flags_ext, regions):
    wide = regions + 2 * REACH
    jkeys = key_ext.reshape(wide, ROWS // KB, KB)
    jmin = jkeys.min(axis=2)
    jmax = jnp.where(jkeys < 0.5 * DEAD, jkeys, -DEAD).max(axis=2)
    ikeys = key_ext.reshape(wide, ROWS // NB, NB)[REACH : REACH + regions]
    imin = ikeys.min(axis=2)
    imax = jnp.where(ikeys < 0.5 * DEAD, ikeys, -DEAD).max(axis=2)
    los, his = [], []
    ids = jnp.arange(ROWS // KB, dtype=jnp.int32)[None, None, :]
    for dh in range(2 * REACH + 1):
        lo_j = jmin[dh : dh + regions]
        hi_j = jmax[dh : dh + regions]
        d = dh - REACH
        if d == 0:
            flag = jnp.ones((regions,), jnp.bool_)
        elif d > 0:
            flag = flags_ext[d - 1, REACH : REACH + regions] > 0.5
        else:
            flag = flags_ext[-d - 1, REACH + d : REACH + d + regions] > 0.5
        near = (
            (hi_j[:, None, :] >= imin[:, :, None] - 1.001)
            & (lo_j[:, None, :] <= imax[:, :, None] + 1.001)
            & (imin[:, :, None] < 0.5 * DEAD)
            & flag[:, None, None]
        )
        los.append(jnp.where(near, ids, ROWS // KB).min(axis=2).reshape(-1))
        his.append(jnp.where(near, ids + 1, 0).max(axis=2).reshape(-1))
    return jnp.stack([jnp.concatenate(los), jnp.concatenate(his)])


def on_device(
    innovation,
    obs_along,
    obs_across,
    obs_scale,
    obs_error,
    obs_gain,
    pair_live,
    obs_count,
    col_owner,
):
    axes = ("reg", "col")
    regions = obs_count.shape[0]
    ens, own = innovation.shape
    live = (
        (jnp.arange(ROWS, dtype=jnp.int32)[None, :] < obs_count[:, None])
        .astype(f32)
        .reshape(own)
    )
    flags = jnp.repeat(pair_live.astype(f32).T, ROWS, axis=1)
    zero = jnp.zeros((own,), f32)
    meta = jnp.stack(
        [obs_along, obs_across, obs_scale * live, obs_error, flags[0], flags[1]]
        + [jnp.where(live > 0.5, obs_across, DEAD)]
        + [zero] * (META - 7)
    )
    total_cols = COLS_DEV * lax.axis_size(axes)
    local_col = (col_owner - lax.axis_index(axes) * COLS_DEV) % total_cols
    info = jnp.stack([obs_gain, live, local_col.astype(f32)] + [zero] * 5)

    first, last, rank = sort_call(innovation, meta)
    after = shift(first, -1)
    before = shift(last, 1)
    chunks = [before, first, last, after]
    innov_cols = innov_columns_call(innovation, info)
    innov_came = shift(innov_cols[:, COLS_DEV:], 1)
    keys = jnp.concatenate([c[ens + 6] for c in chunks])
    flags_ext = jnp.concatenate([c[ens + 4 : ens + 6, ::ROWS] for c in chunks], axis=1)
    bounds = block_bounds(keys, flags_ext, regions)

    imga, imgb, grams, *lists = first_call(bounds, chunks, ens, own)
    img_after = shift(imga, -1)
    img_before = shift(imgb, 1)
    step0, inv0, curv0 = solve_first(sum_all(grams, 0))
    back, img_cols = columns_call(info, rank, imga, imgb)
    img_came = shift(img_cols[:, COLS_DEV:], 1)
    grams = second_call(lists, step0, chunks, [img_before, imga, imgb, img_after], ens, own)
    coef = solve_second(sum_all(grams, 1), step0, inv0, curv0)
    return tuple(
        final_call(coef, innovation, info, back, innov_cols, innov_came, img_cols, img_came)
    )


def solution(mesh):
    one = P(("reg", "col"))
    in_specs = (P(None, ("reg", "col")), one, one, one, one, one, P(("reg", "col"), None), one, one)
    out_specs = (P(None, ("reg", "col")), P(None, ("reg", "col")))
    return jax.shard_map(
        on_device, mesh=mesh, in_specs=in_specs, out_specs=out_specs, check_vma=False
    )
```

```python
import functools

import jax
import jax.numpy as jnp
from jax import lax
from jax.experimental import pallas as pl
from jax.experimental.pallas import tpu as pltpu
from jax.sharding import PartitionSpec as P

ROWS = 1024
REACH = 2
COLS_DEV = 1024
META = 16
KB = 128
NB = 128
UNROLL = 4
DEAD = 1e9
VMEM_LIMIT = 60 * 1024 * 1024

highest = lax.Precision.HIGHEST
f32 = jnp.float32
bf16 = jnp.bfloat16
NT = (((1,), (1,)), ((), ()))
NN = (((1,), (0,)), ((), ()))
TN = (((0,), (0,)), ((), ()))
vmem = pl.BlockSpec(memory_space=pltpu.VMEM)
smem = pl.BlockSpec(memory_space=pltpu.SMEM)


def shift(block, distance):
    axis = ("reg", "col")
    n = lax.axis_size(axis)
    return lax.ppermute(block, axis, [((i - distance) % n, i) for i in range(n)])


def dot(a, b, dims=NN):
    return lax.dot_general(a, b, dims, preferred_element_type=f32)


def two(x):
    hi = x.astype(bf16)
    return hi, (x - hi.astype(f32)).astype(bf16)


def three(x):
    hi = x.astype(bf16)
    rest = x - hi.astype(f32)
    mid = rest.astype(bf16)
    return hi, mid, (rest - mid.astype(f32)).astype(bf16)


def combine(coef_t, blocks):
    chi, clo = two(coef_t)
    bhi, blo = two(blocks)
    return dot(
        jnp.concatenate([chi, chi, clo], axis=1), jnp.concatenate([bhi, blo, bhi], axis=0)
    )


def params():
    return pltpu.CompilerParams(vmem_limit_bytes=VMEM_LIMIT)


def sort_kernel(innov_ref, meta_ref, first_ref, last_ref, rank_ref, own_ref):
    regions = innov_ref.shape[1] // ROWS
    kept = first_ref.shape[0]
    sub = lax.broadcasted_iota(jnp.int32, (ROWS, 128), 0)
    lane = lax.broadcasted_iota(jnp.int32, (ROWS, 128), 1)
    for g in range(regions):
        cols = pl.ds(g * ROWS, ROWS)
        meta = meta_ref[:, cols]
        key = meta[6:7]
        live = (key < 0.5 * DEAD).astype(f32)
        key_col = jnp.broadcast_to(key, (128, ROWS)).T
        ranks = []
        for b in range(ROWS // 128):
            mine = key[:, b * 128 : (b + 1) * 128]
            before = (key_col < mine) | ((key_col == mine) & (sub < lane + b * 128))
            ranks.append(jnp.sum(before.astype(f32), axis=0, keepdims=True))
        rank = jnp.concatenate(ranks, axis=1)
        rank_ref[:, cols] = jnp.broadcast_to(rank, (8, ROWS))
        stack = jnp.concatenate([innov_ref[:, cols] * live, meta], axis=0)
        lhs = jnp.concatenate(three(stack), axis=0)
        n = stack.shape[0]
        rank_i = rank.astype(jnp.int32)
        out_ref = first_ref if g < regions // 2 else last_ref
        for c in range(ROWS // 256):
            slot = lax.broadcasted_iota(jnp.int32, (256, ROWS), 0) + c * 256
            place = (slot == rank_i).astype(f32).astype(bf16)
            got = dot(lhs, place, NT)
            start = (g % (regions // 2)) * ROWS + c * 256
            got = (got[:n] + got[n : 2 * n] + got[2 * n :])[:kept]
            out_ref[:, start : start + 256] = got
            own_ref[:, g * ROWS + c * 256 : g * ROWS + (c + 1) * 256] = got[kept - 8 :]


def sort_call(innov, meta):
    ens, n = innov.shape
    half = jax.ShapeDtypeStruct((ens + 8, n // 2), f32)
    return pl.pallas_call(
        sort_kernel,
        out_shape=(half, half) + (jax.ShapeDtypeStruct((8, n), f32),) * 2,
        in_specs=[vmem, vmem],
        out_specs=(vmem,) * 4,
        compiler_params=params(),
        name="sort_slots",
    )(innov, meta)


def build_list(bounds_ref, list_ref, tile_ref, count_ref, tiles):
    per = ROWS // NB
    zero_block = (tiles // per + 2 * REACH) * (ROWS // KB)

    def one(t, trip):
        g = t // per
        base = trip * UNROLL

        def put(dh, jb, n):
            list_ref[n] = (g + dh) * (ROWS // KB) + jb
            return n + 1

        n = base
        for dh in range(2 * REACH + 1):
            lo = bounds_ref[0, dh * tiles + t]
            hi = bounds_ref[1, dh * tiles + t]
            n = lax.fori_loop(lo, hi, functools.partial(put, dh), n)
        for p in range(UNROLL):
            list_ref[n + p] = zero_block
        end = (n + UNROLL - 1) // UNROLL

        def mark(k, carry):
            tile_ref[k] = t
            return carry

        lax.fori_loop(trip, end, mark, 0)
        return end

    trips = lax.fori_loop(0, tiles, one, 0)
    tile_ref[trips] = 0
    for p in range(UNROLL):
        list_ref[trips * UNROLL + p] = zero_block
    count_ref[0] = trips


def prepare(chunks, row_ref, along_ref, across_ref):
    width = chunks[0].shape[1]
    per = width // ROWS
    for c, ref in enumerate(chunks):
        row_ref[:, c * width : (c + 1) * width] = ref[ref.shape[0] - 8 :, :]
        for r in range(per):
            h = c * per + r
            at = slice(h * ROWS, (h + 1) * ROWS)
            row_ref[0:1, at] = row_ref[0:1, at] + float(h)
            col = row_ref[:, at].T
            along_ref[at, :] = jnp.broadcast_to(col[:, 0:1], (ROWS, NB))
            across_ref[at, :] = jnp.broadcast_to(col[:, 1:2], (ROWS, NB))
    wide = width * len(chunks)
    along_ref[wide : wide + KB, :] = jnp.zeros((KB, NB), f32)
    across_ref[wide : wide + KB, :] = jnp.zeros((KB, NB), f32)


def apply_cov(list_ref, tile_ref, count_ref, row_ref, along_ref, across_ref, v_ref, img_ref, stack_ref, s_ref):
    ens, wide = v_ref.shape
    own = img_ref.shape[1]
    lead = REACH * ROWS
    chunk = 2048
    for c in range(wide // chunk):
        at = pl.ds(c * chunk, chunk)
        hi, lo = two(v_ref[:, at] * row_ref[2:3, at])
        stack_ref[0:ens, at] = hi
        stack_ref[ens : 2 * ens, at] = lo
    stack_ref[:, wide : wide + KB] = jnp.zeros((2 * ens, KB), bf16)
    s_ref[...] = jnp.zeros_like(s_ref)
    img_ref[...] = jnp.zeros_like(img_ref)
    depth = UNROLL * KB

    def step(k, carry):
        before = jnp.maximum(k - 1, 0)
        vhi, vlo = [], []
        for p in range(UNROLL):
            block = list_ref[before * UNROLL + p]
            part = stack_ref[:, pl.ds(pl.multiple_of(block * KB, KB), KB)]
            vhi.append(part[:ens])
            vlo.append(part[ens:])
        lhs = jnp.concatenate(vhi + vlo + vhi, axis=1)
        shi = s_ref[:depth]
        rhs = jnp.concatenate([shi, shi, s_ref[depth:]], axis=0)
        o_at = pl.ds(pl.multiple_of(tile_ref[before] * NB, NB), NB)
        img_ref[:, o_at] += dot(lhs, rhs)
        i_at = pl.ds(pl.multiple_of(lead + tile_ref[k] * NB, NB), NB)
        a_i = row_ref[0:1, i_at]
        b_i = row_ref[1:2, i_at]
        for p in range(UNROLL):
            block = list_ref[k * UNROLL + p]
            j_at = pl.ds(pl.multiple_of(block * KB, KB), KB)
            da = along_ref[j_at, :] - a_i
            db = across_ref[j_at, :] - b_i
            r2 = da * da + db * db
            r = r2 * lax.rsqrt(jnp.maximum(r2, 1e-30))
            u = jnp.maximum(1.0 - r, 0.0)
            u2 = u * u
            hi, lo = two((u2 * u2) * (r + 0.25))
            s_ref[p * KB : (p + 1) * KB] = hi
            s_ref[depth + p * KB : depth + (p + 1) * KB] = lo
        return carry

    lax.fori_loop(0, count_ref[0] + 1, step, 0)
    for c in range(own // chunk):
        at = slice(c * chunk, (c + 1) * chunk)
        e_at = slice(lead + c * chunk, lead + (c + 1) * chunk)
        img_ref[:, at] = (
            img_ref[:, at] * (row_ref[2:3, e_at] * 0.25) + row_ref[3:4, e_at] * v_ref[:, e_at]
        )


def gram(a, b):
    ahi, alo = two(a)
    bhi, blo = two(b)
    return dot(
        jnp.concatenate([ahi, ahi, alo], axis=1), jnp.concatenate([bhi, blo, bhi], axis=1), NT
    )


def first_kernel(
    bounds_ref,
    c0,
    c1,
    c2,
    c3,
    imga_ref,
    imgb_ref,
    gram_ref,
    list_ref,
    tile_ref,
    count_ref,
    row_ref,
    along_ref,
    across_ref,
    v_ref,
    img_ref,
    stack_ref,
    s_ref,
):
    ens, own = img_ref.shape
    lead = REACH * ROWS
    chunks = [c0, c1, c2, c3]
    build_list(bounds_ref, list_ref, tile_ref, count_ref, own // NB)
    prepare(chunks, row_ref, along_ref, across_ref)
    for c, ref in enumerate(chunks):
        v_ref[:, c * lead : (c + 1) * lead] = ref[:ens, :]
    apply_cov(
        list_ref, tile_ref, count_ref, row_ref, along_ref, across_ref, v_ref, img_ref, stack_ref, s_ref
    )
    imga_ref[...] = img_ref[:, :lead]
    imgb_ref[...] = img_ref[:, lead:]
    r = v_ref[:, lead : lead + own]
    gram_ref[...] = gram(r, jnp.concatenate([r, img_ref[...]], axis=0))


def second_kernel(
    list_ref,
    tile_ref,
    count_ref,
    step_ref,
    c0,
    c1,
    c2,
    c3,
    i0,
    i1,
    i2,
    i3,
    gram_ref,
    row_ref,
    along_ref,
    across_ref,
    v_ref,
    img_ref,
    stack_ref,
    s_ref,
):
    ens, own = img_ref.shape
    lead = REACH * ROWS
    chunks = [c0, c1, c2, c3]
    prepare(chunks, row_ref, along_ref, across_ref)
    step_t = step_ref[...].T
    for c, (ref, image) in enumerate(zip(chunks, [i0, i1, i2, i3])):
        v_ref[:, c * lead : (c + 1) * lead] = ref[:ens, :] - combine(step_t, image[...])
    apply_cov(
        list_ref, tile_ref, count_ref, row_ref, along_ref, across_ref, v_ref, img_ref, stack_ref, s_ref
    )
    r = v_ref[:, lead : lead + own]
    gram_ref[:ens] = gram(r, jnp.concatenate([r, img_ref[...]], axis=0))
    mixed = gram(r, jnp.concatenate([i1[...], i2[...]], axis=1))
    gram_ref[ens:] = jnp.concatenate([mixed, mixed], axis=1)


def scratch(ens, own):
    wide = own + 2 * REACH * ROWS
    return [
        pltpu.VMEM((8, wide), f32),
        pltpu.VMEM((wide + KB, NB), f32),
        pltpu.VMEM((wide + KB, NB), f32),
        pltpu.VMEM((ens, wide), f32),
        pltpu.VMEM((ens, own), f32),
        pltpu.VMEM((2 * ens, wide + KB), bf16),
        pltpu.VMEM((2 * UNROLL * KB, NB), bf16),
    ]


def first_call(bounds, chunks, ens, own):
    tiles = own // NB
    trips = tiles * -(-(2 * REACH + 1) * (ROWS // KB) // UNROLL) + 2
    half = jax.ShapeDtypeStruct((ens, own // 2), f32)
    return pl.pallas_call(
        first_kernel,
        out_shape=(
            half,
            half,
            jax.ShapeDtypeStruct((ens, 2 * ens), f32),
            jax.ShapeDtypeStruct((trips * UNROLL,), jnp.int32),
            jax.ShapeDtypeStruct((trips,), jnp.int32),
            jax.ShapeDtypeStruct((1,), jnp.int32),
        ),
        in_specs=[smem] + [vmem] * 4,
        out_specs=(vmem, vmem, vmem, smem, smem, smem),
        scratch_shapes=scratch(ens, own),
        compiler_params=params(),
        name="operate_first",
    )(bounds, *chunks)


def second_call(lists, step, chunks, images, ens, own):
    return pl.pallas_call(
        second_kernel,
        out_shape=jax.ShapeDtypeStruct((2 * ens, 2 * ens), f32),
        in_specs=[smem] * 3 + [vmem] * 9,
        out_specs=vmem,
        scratch_shapes=scratch(ens, own),
        compiler_params=params(),
        name="operate_second",
    )(*lists, step, *chunks, *images)


def flip(me, size):
    return size * (1 - 2 * ((me // size) % 2))


def exchange_steps(total):
    bits = total.bit_length() - 1
    steps = [[1]] if bits % 2 else []
    for k in range(bits % 2, bits, 2):
        steps.append([2**k, 2 ** (k + 1)])
    return steps


def reduce_kernel(steps, n_col, x_ref, out_ref, send, recv, send_sem, recv_sem):
    me = lax.axis_index("reg") * n_col + lax.axis_index("col")
    partners = []
    for sizes in steps:
        others = [me + flip(me, size) for size in sizes]
        if len(sizes) == 2:
            others.append(others[0] + flip(me, sizes[1]))
        partners.append([(other // n_col, other % n_col) for other in others])
    barrier = pltpu.get_barrier_semaphore()
    for group in partners:
        for other in group:
            pl.semaphore_signal(
                barrier, inc=1, device_id=other, device_id_type=pl.DeviceIdType.MESH
            )
    pl.semaphore_wait(barrier, sum(len(group) for group in partners))
    total = x_ref[...]
    slot = 0
    for k, group in enumerate(partners):
        if k:
            send[k] = total
        copies = []
        for p, other in enumerate(group):
            copies.append(
                pltpu.make_async_remote_copy(
                    src_ref=send.at[k] if k else x_ref,
                    dst_ref=recv.at[slot + p],
                    send_sem=send_sem.at[slot + p],
                    recv_sem=recv_sem.at[slot + p],
                    device_id=other,
                    device_id_type=pl.DeviceIdType.MESH,
                )
            )
        for copy in copies:
            copy.start()
        for copy in copies:
            copy.wait()
        total = total + recv[slot]
        if len(group) == 3:
            total = total + (recv[slot + 1] + recv[slot + 2])
        slot += len(group)
    out_ref[...] = total


def sum_all(x, which):
    n_col = lax.axis_size("col")
    steps = exchange_steps(lax.axis_size("reg") * n_col)
    slots = sum(2 ** len(sizes) - 1 for sizes in steps)
    return pl.pallas_call(
        functools.partial(reduce_kernel, steps, n_col),
        out_shape=jax.ShapeDtypeStruct(x.shape, f32),
        in_specs=[vmem],
        out_specs=vmem,
        scratch_shapes=[
            pltpu.VMEM((len(steps),) + x.shape, f32),
            pltpu.VMEM((slots,) + x.shape, f32),
            pltpu.SemaphoreType.DMA((slots,)),
            pltpu.SemaphoreType.DMA((slots,)),
        ],
        compiler_params=pltpu.CompilerParams(collective_id=which, has_side_effects=True),
        name="sum_all",
    )(x)


def symmetric(matrix):
    return 0.5 * (matrix + matrix.T)


def mm(a, b, dims=NN):
    return lax.dot_general(a, b, dims, precision=highest, preferred_element_type=f32)


def eliminate(chains):
    ens, both = chains[0].shape
    rows = lax.broadcasted_iota(jnp.int32, (ens, both), 0)
    for k in range(ens):
        done = []
        for m in chains:
            col = jnp.broadcast_to(m[:, k : k + 1], (ens, both))
            pivot = m[k : k + 1] / col[k : k + 1]
            done.append(jnp.where(rows == k, pivot, m - col * pivot))
        chains = done
    return [m[:, ens:] for m in chains]


def solve_first_kernel(gram_ref, step_ref, inv_ref, curv_ref):
    ens = gram_ref.shape[0]
    norm = symmetric(gram_ref[:, :ens])
    curv = symmetric(gram_ref[:, ens:])
    rows = lax.broadcasted_iota(jnp.int32, (ens, ens), 0)
    eye = (rows == lax.broadcasted_iota(jnp.int32, (ens, ens), 1)).astype(f32)
    step, inv = eliminate(
        [jnp.concatenate([curv, norm], axis=1), jnp.concatenate([norm, eye], axis=1)]
    )
    step_ref[...] = step
    inv_ref[...] = inv
    curv_ref[...] = curv


def solve_second_kernel(gram_ref, step_ref, inv_ref, curv_ref, coef_ref):
    ens = step_ref.shape[0]
    norm = symmetric(gram_ref[:ens, :ens])
    cross = gram_ref[:ens, ens:]
    mixed = gram_ref[ens:, :ens]
    conj = mm(inv_ref[...], norm)
    coupled = mm(mixed, conj)
    quad = mm(conj, mm(curv_ref[...], conj), TN)
    curv = symmetric(cross + coupled + coupled.T + quad)
    (step,) = eliminate([jnp.concatenate([curv, norm], axis=1)])
    step0 = step_ref[...]
    keep = step0 + step + mm(conj, step)
    coef_ref[...] = jnp.concatenate([keep.T, -mm(step0, step).T], axis=1)


def solve_first(grams):
    ens = grams.shape[0]
    small = jax.ShapeDtypeStruct((ens, ens), f32)
    return pl.pallas_call(
        solve_first_kernel,
        out_shape=(small, small, small),
        in_specs=[vmem],
        out_specs=(vmem, vmem, vmem),
        name="solve_first",
    )(grams)


def solve_second(grams, step0, inv0, curv0):
    ens = step0.shape[0]
    return pl.pallas_call(
        solve_second_kernel,
        out_shape=jax.ShapeDtypeStruct((ens, 2 * ens), f32),
        in_specs=[vmem] * 4,
        out_specs=vmem,
        name="solve_second",
    )(grams, step0, inv0, curv0)


def add_columns(stack, owner, cols_ref):
    ens = cols_ref.shape[0]
    for c in range(2 * COLS_DEV // 256):
        slot = lax.broadcasted_iota(jnp.int32, (256, ROWS), 0) + c * 256
        hot = (slot == owner).astype(f32).astype(bf16)
        got = dot(stack, hot, NT)
        part = slice(c * 256, (c + 1) * 256)
        cols_ref[:, part] += got[:ens] + got[ens:]


def innov_columns_kernel(innov_ref, info_ref, cols_ref):
    cols_ref[...] = jnp.zeros_like(cols_ref)

    def one(g, carry):
        at = pl.ds(pl.multiple_of(g * ROWS, ROWS), ROWS)
        scale = info_ref[0:1, at] * info_ref[1:2, at]
        owner = info_ref[2:3, at].astype(jnp.int32)
        add_columns(jnp.concatenate(two(innov_ref[:, at] * scale), axis=0), owner, cols_ref)
        return carry

    lax.fori_loop(0, innov_ref.shape[1] // ROWS, one, 0)


def columns_kernel(info_ref, rank_ref, imga_ref, imgb_ref, back_ref, cols_ref):
    ens, own = back_ref.shape
    half = own // 2
    cols_ref[...] = jnp.zeros_like(cols_ref)
    for g in range(own // ROWS):
        at = slice(g * ROWS, (g + 1) * ROWS)
        rank = rank_ref[0:1, at].astype(jnp.int32)
        img_ref = imga_ref if g * ROWS < half else imgb_ref
        begin = (g * ROWS) % half
        lhs = jnp.concatenate(two(img_ref[:, begin : begin + ROWS]), axis=0)
        total = jnp.zeros((2 * ens, ROWS), f32)
        for c in range(ROWS // 256):
            slot = lax.broadcasted_iota(jnp.int32, (256, ROWS), 0) + c * 256
            place = (slot == rank).astype(f32).astype(bf16)
            total = total + dot(lhs[:, c * 256 : (c + 1) * 256], place)
        image = total[:ens] + total[ens:]
        back_ref[:, at] = image
        owner = info_ref[2:3, at].astype(jnp.int32)
        add_columns(jnp.concatenate(two(image * info_ref[0:1, at]), axis=0), owner, cols_ref)


def innov_columns_call(innov, info):
    ens, own = innov.shape
    return pl.pallas_call(
        innov_columns_kernel,
        out_shape=jax.ShapeDtypeStruct((ens, 2 * COLS_DEV), f32),
        in_specs=[vmem] * 2,
        out_specs=vmem,
        compiler_params=params(),
        cost_estimate=pl.CostEstimate(
            flops=2 * 256 * own * 2048, bytes_accessed=4 << 20, transcendentals=0
        ),
        name="innov_columns",
    )(innov, info)


def columns_call(info, rank, imga, imgb):
    ens, half = imga.shape
    return pl.pallas_call(
        columns_kernel,
        out_shape=(
            jax.ShapeDtypeStruct((ens, 2 * half), f32),
            jax.ShapeDtypeStruct((ens, 2 * COLS_DEV), f32),
        ),
        in_specs=[vmem] * 4,
        out_specs=(vmem, vmem),
        compiler_params=params(),
        cost_estimate=pl.CostEstimate(
            flops=2 * 256 * 2 * half * 3072, bytes_accessed=4 << 20, transcendentals=0
        ),
        name="columns",
    )(info, rank, imga, imgb)


def final_kernel(coef_ref, innov_ref, info_ref, back_ref, rc_ref, rin_ref, ic_ref, iin_ref, w_ref, inc_ref):
    coef = coef_ref[...]
    ens = coef.shape[0]
    own = innov_ref.shape[1]
    chunk = 1024
    first, second = coef[:, :ens], coef[:, ens:]
    for c in range(own // chunk):
        at = pl.ds(c * chunk, chunk)
        live = info_ref[1:2, at]
        w_ref[:, at] = combine(first, innov_ref[:, at] * live) + combine(second, back_ref[:, at])
    inc_ref[...] = combine(first, rc_ref[:, :COLS_DEV] + rin_ref[...]) + combine(
        second, ic_ref[:, :COLS_DEV] + iin_ref[...]
    )


def final_call(coef, innov, info, back, *cols):
    ens, own = innov.shape
    return pl.pallas_call(
        final_kernel,
        out_shape=(
            jax.ShapeDtypeStruct((ens, own), f32),
            jax.ShapeDtypeStruct((ens, COLS_DEV), f32),
        ),
        in_specs=[vmem] * 8,
        out_specs=(vmem, vmem),
        compiler_params=params(),
        name="final",
    )(coef, innov, info, back, *cols)


def block_bounds(key_ext, flags_ext, regions):
    wide = regions + 2 * REACH
    jkeys = key_ext.reshape(wide, ROWS // KB, KB)
    jmin = jkeys.min(axis=2)
    jmax = jnp.where(jkeys < 0.5 * DEAD, jkeys, -DEAD).max(axis=2)
    ikeys = key_ext.reshape(wide, ROWS // NB, NB)[REACH : REACH + regions]
    imin = ikeys.min(axis=2)
    imax = jnp.where(ikeys < 0.5 * DEAD, ikeys, -DEAD).max(axis=2)
    los, his = [], []
    ids = jnp.arange(ROWS // KB, dtype=jnp.int32)[None, None, :]
    for dh in range(2 * REACH + 1):
        lo_j = jmin[dh : dh + regions]
        hi_j = jmax[dh : dh + regions]
        d = dh - REACH
        if d == 0:
            flag = jnp.ones((regions,), jnp.bool_)
        elif d > 0:
            flag = flags_ext[d - 1, REACH : REACH + regions] > 0.5
        else:
            flag = flags_ext[-d - 1, REACH + d : REACH + d + regions] > 0.5
        near = (
            (hi_j[:, None, :] >= imin[:, :, None] - 1.001)
            & (lo_j[:, None, :] <= imax[:, :, None] + 1.001)
            & (imin[:, :, None] < 0.5 * DEAD)
            & flag[:, None, None]
        )
        los.append(jnp.where(near, ids, ROWS // KB).min(axis=2).reshape(-1))
        his.append(jnp.where(near, ids + 1, 0).max(axis=2).reshape(-1))
    return jnp.stack([jnp.concatenate(los), jnp.concatenate(his)])


def on_device(
    innovation,
    obs_along,
    obs_across,
    obs_scale,
    obs_error,
    obs_gain,
    pair_live,
    obs_count,
    col_owner,
):
    axes = ("reg", "col")
    regions = obs_count.shape[0]
    ens, own = innovation.shape
    live = (
        (jnp.arange(ROWS, dtype=jnp.int32)[None, :] < obs_count[:, None])
        .astype(f32)
        .reshape(own)
    )
    flags = jnp.repeat(pair_live.astype(f32).T, ROWS, axis=1)
    zero = jnp.zeros((own,), f32)
    meta = jnp.stack(
        [obs_along, obs_across, obs_scale * live, obs_error, flags[0], flags[1]]
        + [jnp.where(live > 0.5, obs_across, DEAD)]
        + [zero] * (META - 7)
    )
    total_cols = COLS_DEV * lax.axis_size(axes)
    local_col = (col_owner - lax.axis_index(axes) * COLS_DEV) % total_cols
    info = jnp.stack([obs_gain, live, local_col.astype(f32)] + [zero] * 5)

    first, last, rank, own_meta = sort_call(innovation, meta)
    after = shift(first, -1)
    before = shift(last, 1)
    chunks = [before, first, last, after]
    innov_cols = innov_columns_call(innovation, info)
    innov_came = shift(innov_cols[:, COLS_DEV:], 1)
    metas = [before[ens:], own_meta, after[ens:]]
    keys = jnp.concatenate([m[6] for m in metas])
    flags_ext = jnp.concatenate([m[4:6, ::ROWS] for m in metas], axis=1)
    bounds = block_bounds(keys, flags_ext, regions)

    imga, imgb, grams, *lists = first_call(bounds, chunks, ens, own)
    img_after = shift(imga, -1)
    img_before = shift(imgb, 1)
    step0, inv0, curv0 = solve_first(sum_all(grams, 0))
    back, img_cols = columns_call(info, rank, imga, imgb)
    img_came = shift(img_cols[:, COLS_DEV:], 1)
    grams = second_call(lists, step0, chunks, [img_before, imga, imgb, img_after], ens, own)
    coef = solve_second(sum_all(grams, 1), step0, inv0, curv0)
    return tuple(
        final_call(coef, innovation, info, back, innov_cols, innov_came, img_cols, img_came)
    )


def solution(mesh):
    one = P(("reg", "col"))
    in_specs = (P(None, ("reg", "col")), one, one, one, one, one, P(("reg", "col"), None), one, one)
    out_specs = (P(None, ("reg", "col")), P(None, ("reg", "col")))
    return jax.shard_map(
        on_device, mesh=mesh, in_specs=in_specs, out_specs=out_specs, check_vma=False
    )
```

```python
import functools

import jax
import jax.numpy as jnp
from jax import lax
from jax.experimental import pallas as pl
from jax.experimental.pallas import tpu as pltpu
from jax.sharding import PartitionSpec as P

ROWS = 1024
REACH = 2
COLS_DEV = 1024
META = 16
KB = 128
NB = 128
UNROLL = 2
DEAD = 1e9
VMEM_LIMIT = 60 * 1024 * 1024

highest = lax.Precision.HIGHEST
f32 = jnp.float32
bf16 = jnp.bfloat16
NT = (((1,), (1,)), ((), ()))
NN = (((1,), (0,)), ((), ()))
TN = (((0,), (0,)), ((), ()))
vmem = pl.BlockSpec(memory_space=pltpu.VMEM)
smem = pl.BlockSpec(memory_space=pltpu.SMEM)


def shift(block, distance):
    axis = ("reg", "col")
    n = lax.axis_size(axis)
    return lax.ppermute(block, axis, [((i - distance) % n, i) for i in range(n)])


def dot(a, b, dims=NN):
    return lax.dot_general(a, b, dims, preferred_element_type=f32)


def two(x):
    hi = x.astype(bf16)
    return hi, (x - hi.astype(f32)).astype(bf16)


def three(x):
    hi = x.astype(bf16)
    rest = x - hi.astype(f32)
    mid = rest.astype(bf16)
    return hi, mid, (rest - mid.astype(f32)).astype(bf16)


def combine(coef_t, blocks):
    chi, clo = two(coef_t)
    bhi, blo = two(blocks)
    return dot(
        jnp.concatenate([chi, chi, clo], axis=1), jnp.concatenate([bhi, blo, bhi], axis=0)
    )


def params():
    return pltpu.CompilerParams(vmem_limit_bytes=VMEM_LIMIT)


def sort_kernel(innov_ref, meta_ref, first_ref, last_ref, rank_ref, own_ref):
    regions = innov_ref.shape[1] // ROWS
    kept = first_ref.shape[0]
    sub = lax.broadcasted_iota(jnp.int32, (ROWS, 128), 0)
    lane = lax.broadcasted_iota(jnp.int32, (ROWS, 128), 1)
    for g in range(regions):
        cols = pl.ds(g * ROWS, ROWS)
        meta = meta_ref[:, cols]
        key = meta[6:7]
        live = (key < 0.5 * DEAD).astype(f32)
        key_col = jnp.broadcast_to(key, (128, ROWS)).T
        ranks = []
        for b in range(ROWS // 128):
            mine = key[:, b * 128 : (b + 1) * 128]
            before = (key_col < mine) | ((key_col == mine) & (sub < lane + b * 128))
            ranks.append(jnp.sum(before.astype(f32), axis=0, keepdims=True))
        rank = jnp.concatenate(ranks, axis=1)
        rank_ref[:, cols] = jnp.broadcast_to(rank, (8, ROWS))
        stack = jnp.concatenate([innov_ref[:, cols] * live, meta], axis=0)
        lhs = jnp.concatenate(three(stack), axis=0)
        n = stack.shape[0]
        rank_i = rank.astype(jnp.int32)
        out_ref = first_ref if g < regions // 2 else last_ref
        for c in range(ROWS // 256):
            slot = lax.broadcasted_iota(jnp.int32, (256, ROWS), 0) + c * 256
            place = (slot == rank_i).astype(f32).astype(bf16)
            got = dot(lhs, place, NT)
            start = (g % (regions // 2)) * ROWS + c * 256
            got = (got[:n] + got[n : 2 * n] + got[2 * n :])[:kept]
            out_ref[:, start : start + 256] = got
            own_ref[:, g * ROWS + c * 256 : g * ROWS + (c + 1) * 256] = got[kept - 8 :]


def sort_call(innov, meta):
    ens, n = innov.shape
    half = jax.ShapeDtypeStruct((ens + 8, n // 2), f32)
    return pl.pallas_call(
        sort_kernel,
        out_shape=(half, half) + (jax.ShapeDtypeStruct((8, n), f32),) * 2,
        in_specs=[vmem, vmem],
        out_specs=(vmem,) * 4,
        compiler_params=params(),
        name="sort_slots",
    )(innov, meta)


def build_list(bounds_ref, list_ref, tile_ref, count_ref, tiles):
    per = ROWS // NB
    zero_block = (tiles // per + 2 * REACH) * (ROWS // KB)

    def one(t, trip):
        g = t // per
        base = trip * UNROLL

        def put(dh, jb, n):
            list_ref[n] = (g + dh) * (ROWS // KB) + jb
            return n + 1

        n = base
        for dh in range(2 * REACH + 1):
            lo = bounds_ref[0, dh * tiles + t]
            hi = bounds_ref[1, dh * tiles + t]
            n = lax.fori_loop(lo, hi, functools.partial(put, dh), n)
        for p in range(UNROLL):
            list_ref[n + p] = zero_block
        end = (n + UNROLL - 1) // UNROLL

        def mark(k, carry):
            tile_ref[k] = t
            return carry

        lax.fori_loop(trip, end, mark, 0)
        return end

    trips = lax.fori_loop(0, tiles, one, 0)
    tile_ref[trips] = 0
    for p in range(UNROLL):
        list_ref[trips * UNROLL + p] = zero_block
    count_ref[0] = trips


def prepare(chunks, row_ref, along_ref, across_ref):
    width = chunks[0].shape[1]
    per = width // ROWS
    for c, ref in enumerate(chunks):
        row_ref[:, c * width : (c + 1) * width] = ref[ref.shape[0] - 8 :, :]
        for r in range(per):
            h = c * per + r
            at = slice(h * ROWS, (h + 1) * ROWS)
            row_ref[0:1, at] = row_ref[0:1, at] + float(h)
            col = row_ref[:, at].T
            along_ref[at, :] = jnp.broadcast_to(col[:, 0:1], (ROWS, NB))
            across_ref[at, :] = jnp.broadcast_to(col[:, 1:2], (ROWS, NB))
    wide = width * len(chunks)
    along_ref[wide : wide + KB, :] = jnp.zeros((KB, NB), f32)
    across_ref[wide : wide + KB, :] = jnp.zeros((KB, NB), f32)


def apply_cov(list_ref, tile_ref, count_ref, row_ref, along_ref, across_ref, v_ref, img_ref, stack_ref, s_ref):
    ens, wide = v_ref.shape
    own = img_ref.shape[1]
    lead = REACH * ROWS
    chunk = 2048
    for c in range(wide // chunk):
        at = pl.ds(c * chunk, chunk)
        hi, lo = two(v_ref[:, at] * row_ref[2:3, at])
        stack_ref[0:ens, at] = hi
        stack_ref[ens : 2 * ens, at] = lo
    stack_ref[:, wide : wide + KB] = jnp.zeros((2 * ens, KB), bf16)
    s_ref[...] = jnp.zeros_like(s_ref)
    img_ref[...] = jnp.zeros_like(img_ref)
    depth = UNROLL * KB

    def step(k, carry):
        before = jnp.maximum(k - 1, 0)
        vhi, vlo = [], []
        for p in range(UNROLL):
            block = list_ref[before * UNROLL + p]
            part = stack_ref[:, pl.ds(pl.multiple_of(block * KB, KB), KB)]
            vhi.append(part[:ens])
            vlo.append(part[ens:])
        lhs = jnp.concatenate(vhi + vlo + vhi, axis=1)
        shi = s_ref[:depth]
        rhs = jnp.concatenate([shi, shi, s_ref[depth:]], axis=0)
        o_at = pl.ds(pl.multiple_of(tile_ref[before] * NB, NB), NB)
        img_ref[:, o_at] += dot(lhs, rhs)
        i_at = pl.ds(pl.multiple_of(lead + tile_ref[k] * NB, NB), NB)
        a_i = row_ref[0:1, i_at]
        b_i = row_ref[1:2, i_at]
        for p in range(UNROLL):
            block = list_ref[k * UNROLL + p]
            j_at = pl.ds(pl.multiple_of(block * KB, KB), KB)
            da = along_ref[j_at, :] - a_i
            db = across_ref[j_at, :] - b_i
            r2 = da * da + db * db
            r = r2 * lax.rsqrt(jnp.maximum(r2, 1e-30))
            u = jnp.maximum(1.0 - r, 0.0)
            u2 = u * u
            hi, lo = two((u2 * u2) * (r + 0.25))
            s_ref[p * KB : (p + 1) * KB] = hi
            s_ref[depth + p * KB : depth + (p + 1) * KB] = lo
        return carry

    lax.fori_loop(0, count_ref[0] + 1, step, 0)
    for c in range(own // chunk):
        at = slice(c * chunk, (c + 1) * chunk)
        e_at = slice(lead + c * chunk, lead + (c + 1) * chunk)
        img_ref[:, at] = (
            img_ref[:, at] * (row_ref[2:3, e_at] * 0.25) + row_ref[3:4, e_at] * v_ref[:, e_at]
        )


def gram(a, b):
    ahi, alo = two(a)
    bhi, blo = two(b)
    return dot(
        jnp.concatenate([ahi, ahi, alo], axis=1), jnp.concatenate([bhi, blo, bhi], axis=1), NT
    )


def first_kernel(
    bounds_ref,
    c0,
    c1,
    c2,
    c3,
    imga_ref,
    imgb_ref,
    gram_ref,
    list_ref,
    tile_ref,
    count_ref,
    row_ref,
    along_ref,
    across_ref,
    v_ref,
    img_ref,
    stack_ref,
    s_ref,
):
    ens, own = img_ref.shape
    lead = REACH * ROWS
    chunks = [c0, c1, c2, c3]
    build_list(bounds_ref, list_ref, tile_ref, count_ref, own // NB)
    prepare(chunks, row_ref, along_ref, across_ref)
    for c, ref in enumerate(chunks):
        v_ref[:, c * lead : (c + 1) * lead] = ref[:ens, :]
    apply_cov(
        list_ref, tile_ref, count_ref, row_ref, along_ref, across_ref, v_ref, img_ref, stack_ref, s_ref
    )
    imga_ref[...] = img_ref[:, :lead]
    imgb_ref[...] = img_ref[:, lead:]
    r = v_ref[:, lead : lead + own]
    gram_ref[...] = gram(r, jnp.concatenate([r, img_ref[...]], axis=0))


def second_kernel(
    list_ref,
    tile_ref,
    count_ref,
    step_ref,
    c0,
    c1,
    c2,
    c3,
    i0,
    i1,
    i2,
    i3,
    gram_ref,
    row_ref,
    along_ref,
    across_ref,
    v_ref,
    img_ref,
    stack_ref,
    s_ref,
):
    ens, own = img_ref.shape
    lead = REACH * ROWS
    chunks = [c0, c1, c2, c3]
    prepare(chunks, row_ref, along_ref, across_ref)
    step_t = step_ref[...].T
    for c, (ref, image) in enumerate(zip(chunks, [i0, i1, i2, i3])):
        v_ref[:, c * lead : (c + 1) * lead] = ref[:ens, :] - combine(step_t, image[...])
    apply_cov(
        list_ref, tile_ref, count_ref, row_ref, along_ref, across_ref, v_ref, img_ref, stack_ref, s_ref
    )
    r = v_ref[:, lead : lead + own]
    gram_ref[:ens] = gram(r, jnp.concatenate([r, img_ref[...]], axis=0))
    mixed = gram(r, jnp.concatenate([i1[...], i2[...]], axis=1))
    gram_ref[ens:] = jnp.concatenate([mixed, mixed], axis=1)


def scratch(ens, own):
    wide = own + 2 * REACH * ROWS
    return [
        pltpu.VMEM((8, wide), f32),
        pltpu.VMEM((wide + KB, NB), f32),
        pltpu.VMEM((wide + KB, NB), f32),
        pltpu.VMEM((ens, wide), f32),
        pltpu.VMEM((ens, own), f32),
        pltpu.VMEM((2 * ens, wide + KB), bf16),
        pltpu.VMEM((2 * UNROLL * KB, NB), bf16),
    ]


def first_call(bounds, chunks, ens, own):
    tiles = own // NB
    trips = tiles * -(-(2 * REACH + 1) * (ROWS // KB) // UNROLL) + 2
    half = jax.ShapeDtypeStruct((ens, own // 2), f32)
    return pl.pallas_call(
        first_kernel,
        out_shape=(
            half,
            half,
            jax.ShapeDtypeStruct((ens, 2 * ens), f32),
            jax.ShapeDtypeStruct((trips * UNROLL,), jnp.int32),
            jax.ShapeDtypeStruct((trips,), jnp.int32),
            jax.ShapeDtypeStruct((1,), jnp.int32),
        ),
        in_specs=[smem] + [vmem] * 4,
        out_specs=(vmem, vmem, vmem, smem, smem, smem),
        scratch_shapes=scratch(ens, own),
        compiler_params=params(),
        name="operate_first",
    )(bounds, *chunks)


def second_call(lists, step, chunks, images, ens, own):
    return pl.pallas_call(
        second_kernel,
        out_shape=jax.ShapeDtypeStruct((2 * ens, 2 * ens), f32),
        in_specs=[smem] * 3 + [vmem] * 9,
        out_specs=vmem,
        scratch_shapes=scratch(ens, own),
        compiler_params=params(),
        name="operate_second",
    )(*lists, step, *chunks, *images)


def flip(me, size):
    return size * (1 - 2 * ((me // size) % 2))


def exchange_steps(total):
    bits = total.bit_length() - 1
    steps = [[1]] if bits % 2 else []
    for k in range(bits % 2, bits, 2):
        steps.append([2**k, 2 ** (k + 1)])
    return steps


def reduce_kernel(steps, n_col, x_ref, out_ref, send, recv, send_sem, recv_sem):
    me = lax.axis_index("reg") * n_col + lax.axis_index("col")
    partners = []
    for sizes in steps:
        others = [me + flip(me, size) for size in sizes]
        if len(sizes) == 2:
            others.append(others[0] + flip(me, sizes[1]))
        partners.append([(other // n_col, other % n_col) for other in others])
    barrier = pltpu.get_barrier_semaphore()
    for group in partners:
        for other in group:
            pl.semaphore_signal(
                barrier, inc=1, device_id=other, device_id_type=pl.DeviceIdType.MESH
            )
    pl.semaphore_wait(barrier, sum(len(group) for group in partners))
    total = x_ref[...]
    slot = 0
    for k, group in enumerate(partners):
        if k:
            send[k] = total
        copies = []
        for p, other in enumerate(group):
            copies.append(
                pltpu.make_async_remote_copy(
                    src_ref=send.at[k] if k else x_ref,
                    dst_ref=recv.at[slot + p],
                    send_sem=send_sem.at[slot + p],
                    recv_sem=recv_sem.at[slot + p],
                    device_id=other,
                    device_id_type=pl.DeviceIdType.MESH,
                )
            )
        for copy in copies:
            copy.start()
        for copy in copies:
            copy.wait()
        total = total + recv[slot]
        if len(group) == 3:
            total = total + (recv[slot + 1] + recv[slot + 2])
        slot += len(group)
    out_ref[...] = total


def sum_all(x, which):
    n_col = lax.axis_size("col")
    steps = exchange_steps(lax.axis_size("reg") * n_col)
    slots = sum(2 ** len(sizes) - 1 for sizes in steps)
    return pl.pallas_call(
        functools.partial(reduce_kernel, steps, n_col),
        out_shape=jax.ShapeDtypeStruct(x.shape, f32),
        in_specs=[vmem],
        out_specs=vmem,
        scratch_shapes=[
            pltpu.VMEM((len(steps),) + x.shape, f32),
            pltpu.VMEM((slots,) + x.shape, f32),
            pltpu.SemaphoreType.DMA((slots,)),
            pltpu.SemaphoreType.DMA((slots,)),
        ],
        compiler_params=pltpu.CompilerParams(collective_id=which, has_side_effects=True),
        name="sum_all",
    )(x)


def symmetric(matrix):
    return 0.5 * (matrix + matrix.T)


def mm(a, b, dims=NN):
    return lax.dot_general(a, b, dims, precision=highest, preferred_element_type=f32)


def eliminate(chains):
    ens, both = chains[0].shape
    rows = lax.broadcasted_iota(jnp.int32, (ens, both), 0)
    for k in range(ens):
        done = []
        for m in chains:
            col = jnp.broadcast_to(m[:, k : k + 1], (ens, both))
            pivot = m[k : k + 1] / col[k : k + 1]
            done.append(jnp.where(rows == k, pivot, m - col * pivot))
        chains = done
    return [m[:, ens:] for m in chains]


def solve_first_kernel(gram_ref, step_ref, inv_ref, curv_ref):
    ens = gram_ref.shape[0]
    norm = symmetric(gram_ref[:, :ens])
    curv = symmetric(gram_ref[:, ens:])
    rows = lax.broadcasted_iota(jnp.int32, (ens, ens), 0)
    eye = (rows == lax.broadcasted_iota(jnp.int32, (ens, ens), 1)).astype(f32)
    step, inv = eliminate(
        [jnp.concatenate([curv, norm], axis=1), jnp.concatenate([norm, eye], axis=1)]
    )
    step_ref[...] = step
    inv_ref[...] = inv
    curv_ref[...] = curv


def solve_second_kernel(gram_ref, step_ref, inv_ref, curv_ref, coef_ref):
    ens = step_ref.shape[0]
    norm = symmetric(gram_ref[:ens, :ens])
    cross = gram_ref[:ens, ens:]
    mixed = gram_ref[ens:, :ens]
    conj = mm(inv_ref[...], norm)
    coupled = mm(mixed, conj)
    quad = mm(conj, mm(curv_ref[...], conj), TN)
    curv = symmetric(cross + coupled + coupled.T + quad)
    (step,) = eliminate([jnp.concatenate([curv, norm], axis=1)])
    step0 = step_ref[...]
    keep = step0 + step + mm(conj, step)
    coef_ref[...] = jnp.concatenate([keep.T, -mm(step0, step).T], axis=1)


def solve_first(grams):
    ens = grams.shape[0]
    small = jax.ShapeDtypeStruct((ens, ens), f32)
    return pl.pallas_call(
        solve_first_kernel,
        out_shape=(small, small, small),
        in_specs=[vmem],
        out_specs=(vmem, vmem, vmem),
        name="solve_first",
    )(grams)


def solve_second(grams, step0, inv0, curv0):
    ens = step0.shape[0]
    return pl.pallas_call(
        solve_second_kernel,
        out_shape=jax.ShapeDtypeStruct((ens, 2 * ens), f32),
        in_specs=[vmem] * 4,
        out_specs=vmem,
        name="solve_second",
    )(grams, step0, inv0, curv0)


def add_columns(stack, owner, cols_ref):
    ens = cols_ref.shape[0]
    for c in range(2 * COLS_DEV // 256):
        slot = lax.broadcasted_iota(jnp.int32, (256, ROWS), 0) + c * 256
        hot = (slot == owner).astype(f32).astype(bf16)
        got = dot(stack, hot, NT)
        part = slice(c * 256, (c + 1) * 256)
        cols_ref[:, part] += got[:ens] + got[ens:]


def innov_columns_kernel(innov_ref, info_ref, cols_ref):
    cols_ref[...] = jnp.zeros_like(cols_ref)

    def one(g, carry):
        at = pl.ds(pl.multiple_of(g * ROWS, ROWS), ROWS)
        scale = info_ref[0:1, at] * info_ref[1:2, at]
        owner = info_ref[2:3, at].astype(jnp.int32)
        add_columns(jnp.concatenate(two(innov_ref[:, at] * scale), axis=0), owner, cols_ref)
        return carry

    lax.fori_loop(0, innov_ref.shape[1] // ROWS, one, 0)


def columns_kernel(info_ref, rank_ref, imga_ref, imgb_ref, back_ref, cols_ref):
    ens, own = back_ref.shape
    half = own // 2
    cols_ref[...] = jnp.zeros_like(cols_ref)
    for g in range(own // ROWS):
        at = slice(g * ROWS, (g + 1) * ROWS)
        rank = rank_ref[0:1, at].astype(jnp.int32)
        img_ref = imga_ref if g * ROWS < half else imgb_ref
        begin = (g * ROWS) % half
        lhs = jnp.concatenate(two(img_ref[:, begin : begin + ROWS]), axis=0)
        total = jnp.zeros((2 * ens, ROWS), f32)
        for c in range(ROWS // 256):
            slot = lax.broadcasted_iota(jnp.int32, (256, ROWS), 0) + c * 256
            place = (slot == rank).astype(f32).astype(bf16)
            total = total + dot(lhs[:, c * 256 : (c + 1) * 256], place)
        image = total[:ens] + total[ens:]
        back_ref[:, at] = image
        owner = info_ref[2:3, at].astype(jnp.int32)
        add_columns(jnp.concatenate(two(image * info_ref[0:1, at]), axis=0), owner, cols_ref)


def innov_columns_call(innov, info):
    ens, own = innov.shape
    return pl.pallas_call(
        innov_columns_kernel,
        out_shape=jax.ShapeDtypeStruct((ens, 2 * COLS_DEV), f32),
        in_specs=[vmem] * 2,
        out_specs=vmem,
        compiler_params=params(),
        cost_estimate=pl.CostEstimate(
            flops=2 * 256 * own * 2048, bytes_accessed=4 << 20, transcendentals=0
        ),
        name="innov_columns",
    )(innov, info)


def columns_call(info, rank, imga, imgb):
    ens, half = imga.shape
    return pl.pallas_call(
        columns_kernel,
        out_shape=(
            jax.ShapeDtypeStruct((ens, 2 * half), f32),
            jax.ShapeDtypeStruct((ens, 2 * COLS_DEV), f32),
        ),
        in_specs=[vmem] * 4,
        out_specs=(vmem, vmem),
        compiler_params=params(),
        cost_estimate=pl.CostEstimate(
            flops=2 * 256 * 2 * half * 3072, bytes_accessed=4 << 20, transcendentals=0
        ),
        name="columns",
    )(info, rank, imga, imgb)


def final_kernel(coef_ref, innov_ref, info_ref, back_ref, rc_ref, rin_ref, ic_ref, iin_ref, w_ref, inc_ref):
    coef = coef_ref[...]
    ens = coef.shape[0]
    own = innov_ref.shape[1]
    chunk = 1024
    first, second = coef[:, :ens], coef[:, ens:]
    for c in range(own // chunk):
        at = pl.ds(c * chunk, chunk)
        live = info_ref[1:2, at]
        w_ref[:, at] = combine(first, innov_ref[:, at] * live) + combine(second, back_ref[:, at])
    inc_ref[...] = combine(first, rc_ref[:, :COLS_DEV] + rin_ref[...]) + combine(
        second, ic_ref[:, :COLS_DEV] + iin_ref[...]
    )


def final_call(coef, innov, info, back, *cols):
    ens, own = innov.shape
    return pl.pallas_call(
        final_kernel,
        out_shape=(
            jax.ShapeDtypeStruct((ens, own), f32),
            jax.ShapeDtypeStruct((ens, COLS_DEV), f32),
        ),
        in_specs=[vmem] * 8,
        out_specs=(vmem, vmem),
        compiler_params=params(),
        name="final",
    )(coef, innov, info, back, *cols)


def block_bounds(key_ext, flags_ext, regions):
    wide = regions + 2 * REACH
    jkeys = key_ext.reshape(wide, ROWS // KB, KB)
    jmin = jkeys.min(axis=2)
    jmax = jnp.where(jkeys < 0.5 * DEAD, jkeys, -DEAD).max(axis=2)
    ikeys = key_ext.reshape(wide, ROWS // NB, NB)[REACH : REACH + regions]
    imin = ikeys.min(axis=2)
    imax = jnp.where(ikeys < 0.5 * DEAD, ikeys, -DEAD).max(axis=2)
    los, his = [], []
    ids = jnp.arange(ROWS // KB, dtype=jnp.int32)[None, None, :]
    for dh in range(2 * REACH + 1):
        lo_j = jmin[dh : dh + regions]
        hi_j = jmax[dh : dh + regions]
        d = dh - REACH
        if d == 0:
            flag = jnp.ones((regions,), jnp.bool_)
        elif d > 0:
            flag = flags_ext[d - 1, REACH : REACH + regions] > 0.5
        else:
            flag = flags_ext[-d - 1, REACH + d : REACH + d + regions] > 0.5
        near = (
            (hi_j[:, None, :] >= imin[:, :, None] - 1.001)
            & (lo_j[:, None, :] <= imax[:, :, None] + 1.001)
            & (imin[:, :, None] < 0.5 * DEAD)
            & flag[:, None, None]
        )
        los.append(jnp.where(near, ids, ROWS // KB).min(axis=2).reshape(-1))
        his.append(jnp.where(near, ids + 1, 0).max(axis=2).reshape(-1))
    return jnp.stack([jnp.concatenate(los), jnp.concatenate(his)])


def on_device(
    innovation,
    obs_along,
    obs_across,
    obs_scale,
    obs_error,
    obs_gain,
    pair_live,
    obs_count,
    col_owner,
):
    axes = ("reg", "col")
    regions = obs_count.shape[0]
    ens, own = innovation.shape
    live = (
        (jnp.arange(ROWS, dtype=jnp.int32)[None, :] < obs_count[:, None])
        .astype(f32)
        .reshape(own)
    )
    flags = jnp.repeat(pair_live.astype(f32).T, ROWS, axis=1)
    zero = jnp.zeros((own,), f32)
    meta = jnp.stack(
        [obs_along, obs_across, obs_scale * live, obs_error, flags[0], flags[1]]
        + [jnp.where(live > 0.5, obs_across, DEAD)]
        + [zero] * (META - 7)
    )
    total_cols = COLS_DEV * lax.axis_size(axes)
    local_col = (col_owner - lax.axis_index(axes) * COLS_DEV) % total_cols
    info = jnp.stack([obs_gain, live, local_col.astype(f32)] + [zero] * 5)

    first, last, rank, own_meta = sort_call(innovation, meta)
    after = shift(first, -1)
    before = shift(last, 1)
    chunks = [before, first, last, after]
    innov_cols = innov_columns_call(innovation, info)
    innov_came = shift(innov_cols[:, COLS_DEV:], 1)
    metas = [before[ens:], own_meta, after[ens:]]
    keys = jnp.concatenate([m[6] for m in metas])
    flags_ext = jnp.concatenate([m[4:6, ::ROWS] for m in metas], axis=1)
    bounds = block_bounds(keys, flags_ext, regions)

    imga, imgb, grams, *lists = first_call(bounds, chunks, ens, own)
    img_after = shift(imga, -1)
    img_before = shift(imgb, 1)
    step0, inv0, curv0 = solve_first(sum_all(grams, 0))
    back, img_cols = columns_call(info, rank, imga, imgb)
    img_came = shift(img_cols[:, COLS_DEV:], 1)
    grams = second_call(lists, step0, chunks, [img_before, imga, imgb, img_after], ens, own)
    coef = solve_second(sum_all(grams, 1), step0, inv0, curv0)
    return tuple(
        final_call(coef, innovation, info, back, innov_cols, innov_came, img_cols, img_came)
    )


def solution(mesh):
    one = P(("reg", "col"))
    in_specs = (P(None, ("reg", "col")), one, one, one, one, one, P(("reg", "col"), None), one, one)
    out_specs = (P(None, ("reg", "col")), P(None, ("reg", "col")))
    return jax.shard_map(
        on_device, mesh=mesh, in_specs=in_specs, out_specs=out_specs, check_vma=False
    )
```
